128 devices in a mesh: dp: 16 (over z_lo, x, core), mp: 8 (over y, z_hi).
Axes of the slice: x: 4, y: 4, z: 4 (z_hi: 2, z_lo: 2; z = z_hi * 2 + z_lo), core: 2. Of those that a mesh axis runs over, the one named last changes fastest.
Arguments:
- fields: bfloat16 [16, 128, 20, 128, 128], P('dp', 'mp'), may hold values from -6 to 6
- cotangent: bfloat16 [16, 128, 20, 128, 128], P('dp', 'mp'), may hold values from -3 to 3
- spectral_weight: bfloat16 [32, 2, 20, 20, 512], P('dp', None, None, None, 'mp'), may hold values from -5 to 5
- conv_weight: bfloat16 [20, 20], replicated, may hold values from -1.25 to 1.25
- conv_bias: float32 [20], replicated, may hold values from -3 to 3
Outputs:
- spectral_grad: float32 [32, 2, 20, 20, 512], P('dp', None, None, None, 'mp')
The draws below stay inside these ranges and needn't reach their ends.
All inputs are finite; a program needn't handle non-finite values.
Results may differ from the reference program's by a relative error of at most 0.0085.
Values may be sent and summed in bfloat16 or wider, within the bound.
No kernel may reach another device: no remote copies, remote signals or barrier semaphores. Data moves between devices by JAX's collectives and lax.ppermute only.
A program may use at most 256 MiB of HBM per device.

```python
import math
import jax
import jax.numpy as jnp
from jax import lax

X = 128
Y = 128
Z = 128
C = 20
KX = 32
KY = 32
KZ = 16
SAMPLES = 16


def block_levels(own_key, shape, shards, least, top_value):
    def one(position, shards_of):
        steps = jax.random.uniform(jax.random.fold_in(jax.random.fold_in(own_key, 6), position), (shards_of,), jnp.float32, least / len(shards), top_value / len(shards))
        return jnp.repeat(jnp.exp(steps), shape[position] // shards_of).reshape((-1,) + (1,) * (len(shape) - position - 1))

    gain = one(*shards[0])
    for cut in shards[1:]:
        gain = gain * one(*cut)
    return gain


def centred(key, extent, spread, most, shards=(), held_as=jnp.bfloat16):
    gain = block_levels(key, extent, shards, -0.22, 0.18) if shards else 1.0
    drawn = jax.random.normal(key, extent, jnp.float32) * spread * gain
    return jnp.minimum(jnp.maximum(drawn, -most), most).astype(held_as)


def setup_inputs(seed: int = 0) -> dict:
    splits = jax.random.split(jax.random.key(seed), 6)
    fields = centred(splits[0], (SAMPLES, X, C, Y, Z), 1.0, 6.0, ((0, 16), (1, 8)))
    cotangent = centred(splits[1], (SAMPLES, X, C, Y, Z), 0.5, 3.0, ((0, 16), (1, 8)))
    spectral_weight = centred(splits[2], (KX, 2, C, C, KY * KZ), 1.0, 5.0, ((0, 16), (4, 8)))
    conv_weight = centred(splits[3], (C, C), C ** -0.5, 1.25)
    conv_bias = centred(splits[4], (C,), 0.5, 3.0, (), jnp.float32)
    return dict(fields=fields, cotangent=cotangent, spectral_weight=spectral_weight, conv_weight=conv_weight, conv_bias=conv_bias)


inv_root_two = 0.7071067811865476
inv_root_two_pi = 0.3989422804014327


def kept_modes(count, length):
    indices = jnp.arange(count, dtype=jnp.int32)
    return jnp.where(indices < count // 2, indices, length - count + indices).astype(jnp.int32)


def gelu_slope(values):
    return 0.5 * (1.0 + lax.erf(values * inv_root_two)) + values * jnp.exp(-0.5 * values * values) * inv_root_two_pi


def reference(fields, cotangent, spectral_weight, conv_weight, conv_bias):
    highest = lax.Precision.HIGHEST
    rows_x = kept_modes(KX, X)
    rows_y = kept_modes(KY, Y)
    modes_z = jnp.arange(KZ, dtype=jnp.int32)
    cells_z = jnp.arange(Z, dtype=jnp.int32)
    phases = (2.0 * math.pi / Z) * ((modes_z[:, None] * cells_z[None, :]) % Z).astype(jnp.float32)
    weight_z = jnp.where(modes_z == 0, 1.0, 2.0).astype(jnp.float32)
    cos_z = weight_z[:, None] * jnp.cos(phases) / Z
    sin_z = weight_z[:, None] * jnp.sin(phases) / Z
    scale_back = weight_z / (X * Y * Z)
    weights = spectral_weight.astype(jnp.float32).reshape(KX, 2, C, C, KY, KZ)
    real_w = weights[:, 0]
    imag_w = weights[:, 1]
    mixing = conv_weight.astype(jnp.float32)

    def truncate(volume):
        full_spec = jnp.fft.rfftn(volume, axes=(0, 2, 3))
        kept_spec = full_spec[rows_x][:, :, rows_y][..., :KZ]
        return jnp.real(kept_spec).astype(jnp.float32), jnp.imag(kept_spec).astype(jnp.float32)

    def place(values):
        section = jnp.zeros((X, C, KY, KZ), jnp.float32).at[rows_x].set(values)
        return jnp.zeros((X, C, Y, KZ), jnp.float32).at[:, :, rows_y].set(section)

    def one_sample(total, inputs):
        sample, cot_sample = inputs
        volume = sample.astype(jnp.float32)
        spec_re, spec_im = truncate(volume)
        mixed_re = jnp.einsum('acbd,acobd->aobd', spec_re, real_w, precision=highest) - jnp.einsum('acbd,acobd->aobd', spec_im, imag_w, precision=highest)
        mixed_im = jnp.einsum('acbd,acobd->aobd', spec_re, imag_w, precision=highest) + jnp.einsum('acbd,acobd->aobd', spec_im, real_w, precision=highest)
        spectrum = place(mixed_re) + 1j * place(mixed_im)
        inverse_xy = jnp.fft.ifft2(spectrum, axes=(0, 2))
        spectral = jnp.einsum('xoyk,kz->xoyz', jnp.real(inverse_xy).astype(jnp.float32), cos_z, precision=highest) - jnp.einsum('xoyk,kz->xoyz', jnp.imag(inverse_xy).astype(jnp.float32), sin_z, precision=highest)
        conv_term = jnp.einsum('xcyz,co->xoyz', volume, mixing, precision=highest)
        pre_act = spectral + conv_term + conv_bias[None, :, None, None]
        grad_pre = (cot_sample.astype(jnp.float32) * gelu_slope(pre_act)).astype(jnp.bfloat16)
        back_re, back_im = truncate(grad_pre.astype(jnp.float32))
        back_re = back_re * scale_back
        back_im = back_im * scale_back
        grad_re = jnp.einsum('acbd,aobd->acobd', spec_re, back_re, precision=highest) + jnp.einsum('acbd,aobd->acobd', spec_im, back_im, precision=highest)
        grad_im = jnp.einsum('acbd,aobd->acobd', spec_re, back_im, precision=highest) - jnp.einsum('acbd,aobd->acobd', spec_im, back_re, precision=highest)
        term = jnp.stack([grad_re, grad_im], axis=1).reshape(KX, 2, C, C, KY * KZ)
        return total + term, None

    start_total = jnp.zeros((KX, 2, C, C, KY * KZ), jnp.float32)
    result, unused = lax.scan(one_sample, start_total, (fields, cotangent))
    return result
```

```python
import functools

import jax
import jax.numpy as jnp
import ml_dtypes
import numpy as np
from jax import lax
from jax.experimental import pallas as pl
from jax.experimental.pallas import tpu as pltpu
from jax.sharding import PartitionSpec as P

X = 128
Y = 128
Z = 128
C = 20
KX = 32
KY = 32
KZ = 16
DP = 16
MP = 8
XP = 8
G = 5
GK = 20
GA = 10

bf16 = jnp.bfloat16
f32 = jnp.float32
np_bf16 = ml_dtypes.bfloat16

INV_ROOT_TWO = 0.7071067811865476
INV_ROOT_TWO_PI = 0.3989422804014327


def kept(count, length):
    return np.concatenate([np.arange(count // 2), np.arange(length - count // 2, length)])


def angles(modes, length):
    return 2.0 * np.pi / length * ((modes[:, None] * np.arange(length)[None, :]) % length)


def hi_lo(table):
    upper = table.astype(np_bf16)
    lower = (table - upper.astype(np.float64)).astype(np_bf16)
    return upper, lower


def z_scales():
    candidates = 1.0 + np.arange(512) / 512
    scales = []
    for row in angles(np.arange(KZ), Z):
        values = np.concatenate([np.cos(row), np.sin(row)])[None, :] * candidates[:, None]
        off = ((values.astype(np_bf16).astype(np.float64) - values) ** 2).sum(1) / (values**2).sum(1)
        scales.append(candidates[int(np.argmin(off))])
    return np.array(scales)


@functools.cache
def tables():
    scale = z_scales()
    weight = np.where(np.arange(KZ) == 0, 1.0, 2.0) / (X * Y * Z)
    phase_z = angles(np.arange(KZ), Z)
    cos_z, sin_z = np.cos(phase_z), np.sin(phase_z)
    forward_z = np.zeros((8, Z, 2, 8, KZ))
    inverse_z = np.zeros((4, 2, 8, KZ, 2, Z))
    for q in range(8):
        forward_z[q, :, 0, q, :] = (cos_z * scale[:, None]).T
        forward_z[q, :, 1, q, :] = (sin_z * scale[:, None]).T
        inverse_z[q // 2, 0, q, :, q % 2, :] = cos_z * scale[:, None]
        inverse_z[q // 2, 1, q, :, q % 2, :] = -sin_z * scale[:, None]
    unscale = np.tile(1.0 / scale, 16)[None, :]
    unscale_back = np.tile(weight / scale, 16)[None, :]
    unscale_inverse = np.tile(weight / scale, 8)[None, :]
    phase_y = angles(kept(KY, Y), Y)
    cos_y, sin_y = np.cos(phase_y), np.sin(phase_y)
    forward_y = np.zeros((KY, 2, 2, Y))
    forward_y[:, 0, 0], forward_y[:, 0, 1] = cos_y, -sin_y
    forward_y[:, 1, 0], forward_y[:, 1, 1] = -sin_y, -cos_y
    forward_y = np.concatenate(hi_lo(forward_y.reshape(64, 256)), axis=0)
    inverse_y = np.zeros((2, Y, KY, 2))
    inverse_y[0, :, :, 0], inverse_y[0, :, :, 1] = cos_y.T, -sin_y.T
    inverse_y[1, :, :, 0], inverse_y[1, :, :, 1] = sin_y.T, cos_y.T
    inverse_y = np.concatenate(hi_lo(inverse_y.reshape(256, 64)), axis=1)
    phase_x = angles(kept(KX, X), X).reshape(16, 2, 8, 8, 2)
    cos_x, sin_x = np.cos(phase_x), np.sin(phase_x)
    forward_x = np.zeros((2, 2, 2, 16, 8, 2, 8))
    inverse_x = np.zeros((2, 8, 2, 8, 2, 2, 16))
    cos_f = np.transpose(cos_x, (4, 1, 0, 2, 3))
    sin_f = np.transpose(sin_x, (4, 1, 0, 2, 3))
    forward_x[:, :, 0, :, :, 0, :] = cos_f
    forward_x[:, :, 0, :, :, 1, :] = sin_f
    forward_x[:, :, 1, :, :, 0, :] = -sin_f
    forward_x[:, :, 1, :, :, 1, :] = cos_f
    cos_i = np.transpose(cos_x, (4, 2, 3, 1, 0))
    sin_i = np.transpose(sin_x, (4, 2, 3, 1, 0))
    inverse_x[:, :, 0, :, :, 0, :] = cos_i
    inverse_x[:, :, 0, :, :, 1, :] = -sin_i
    inverse_x[:, :, 1, :, :, 0, :] = sin_i
    inverse_x[:, :, 1, :, :, 1, :] = cos_i
    forward_x = np.concatenate(hi_lo(forward_x.reshape(128, 128)), axis=1)
    inverse_x = np.concatenate(hi_lo(inverse_x.reshape(256, 64)), axis=1)
    spread = np.zeros((2, 4, KZ, 4, 2, 4, KZ))
    for channel in range(4):
        for place in range(4):
            for b in range(2):
                spread[b, channel, np.arange(KZ), channel, b, place, np.arange(KZ)] = 1.0
    spread = spread.reshape(128, 512)
    spread = np.concatenate([spread, spread], axis=0)
    place = np.zeros((4, 4, KZ, 2, 2, 4, KZ))
    for o in range(4):
        for kyl in range(4):
            place[o, kyl, np.arange(KZ), kyl // 2, kyl % 2, o, np.arange(KZ)] = 1.0
    return dict(
        forward_z=forward_z.reshape(4, 256, 256).astype(np_bf16),
        inverse_z=inverse_z.reshape(4, 256, 256).astype(np_bf16),
        unscale=unscale.astype(np.float32),
        unscale_back=unscale_back.astype(np.float32),
        unscale_inverse=unscale_inverse.astype(np.float32),
        forward_y=forward_y,
        inverse_y=inverse_y,
        forward_x=forward_x,
        inverse_x=inverse_x,
        spread=spread.astype(np_bf16),
        place=place.reshape(256, 256).astype(np_bf16),
    )


def mm(a, b):
    return jnp.dot(a, b, preferred_element_type=f32)


def analyse(lhs_of_pair, fz_ref, fy_ref, un_ref, modes_ref, step):
    total = mm(lhs_of_pair(0), fz_ref[0])
    for pair in range(1, 4):
        total = total + mm(lhs_of_pair(pair), fz_ref[pair])
    total = total * un_ref[...]
    for g in range(G):
        part = total[g * Y : (g + 1) * Y]
        both = jnp.concatenate([part[:, :128], part[:, 128:]], axis=0)
        upper = both.astype(bf16)
        lower = (both - upper.astype(f32)).astype(bf16)
        out = mm(fy_ref[...], jnp.concatenate([upper, lower], axis=1))
        modes = out[:64, :128] + out[64:, :128] + out[:64, 128:]
        for j in range(MP):
            modes_ref[pl.ds(j * 320 + g * 64 + step, 8, stride=8), :] = modes[j * 8 : (j + 1) * 8]


def analyse_kernel(field_ref, fz_ref, fy_ref, un_ref, out_ref, modes_ref):
    step = pl.program_id(0)

    def lhs(pair):
        xl, c4 = pair // 2, 2 * (pair % 2)
        rows = [
            jnp.concatenate(
                [field_ref[0, xl, 4 * g + c4], field_ref[0, xl, 4 * g + c4 + 1]], axis=1
            )
            for g in range(G)
        ]
        return jnp.concatenate(rows, axis=0)

    analyse(lhs, fz_ref, fy_ref, un_ref, modes_ref, step)

    @pl.when(step == XP - 1)
    def _():
        out_ref[...] = modes_ref[...].astype(bf16)


def full(shape):
    zeros = (0,) * len(shape)
    return pl.BlockSpec(shape, lambda *_: zeros, pipeline_mode=pl.Buffered(1))


def analyse_call(fields, t):
    return pl.pallas_call(
        analyse_kernel,
        out_shape=jax.ShapeDtypeStruct((2560, 128), bf16),
        grid=(XP,),
        in_specs=[
            pl.BlockSpec((1, 2, C, Y, Z), lambda i: (0, i, 0, 0, 0)),
            full((4, 256, 256)),
            full((128, 256)),
            full((1, 256)),
        ],
        out_specs=pl.BlockSpec((2560, 128), lambda i: (0, 0)),
        scratch_shapes=[pltpu.VMEM((2560, 128), f32)],
        compiler_params=pltpu.CompilerParams(
            dimension_semantics=("arbitrary",), vmem_limit_bytes=60 << 20
        ),
        name="analyse",
    )(fields, t["forward_z"], t["forward_y"], t["unscale"])


def gelu_slope(values):
    return (
        0.5 * (1.0 + lax.erf(values * INV_ROOT_TWO))
        + values * jnp.exp(-0.5 * values * values) * INV_ROOT_TWO_PI
    )


def slab_kernel(
    field_ref, cot_ref, mixed_ref, conv_ref, bias_ref, iy_ref, iz_ref, uni_ref, fz_ref, fy_ref, un_ref,
    out_ref, modes_ref, mixed_f32, conv_out, wave_ref, delta_ref,
):
    step = pl.program_id(0)

    @pl.when(step == 0)
    def _():
        mixed_f32[...] = mixed_ref[...].astype(f32)

    for g in range(G):
        rows = [mixed_f32[pl.ds(j * 320 + g * 64 + step, 8, stride=8), :] for j in range(MP)]
        part = jnp.concatenate(rows, axis=0).astype(bf16)
        wave = mm(iy_ref[...], jnp.concatenate([part, part], axis=0))
        wave = (wave * uni_ref[...]).astype(bf16)
        wave_ref[g * Y : (g + 1) * Y, :128] = wave[:Y]
        wave_ref[g * Y : (g + 1) * Y, 128:] = wave[Y:]

    for xl in range(2):
        for yp in range(4):
            right = jnp.concatenate(
                [
                    field_ref[0, xl, :, yp * 32 + h * 16 : yp * 32 + (h + 1) * 16, :].reshape(320, Z)
                    for h in range(2)
                ],
                axis=1,
            )
            out = mm(conv_ref[...], right)
            for h in range(2):
                conv_out[:, yp * 32 + h * 16 : yp * 32 + (h + 1) * 16, :] = out[
                    :, h * 128 : (h + 1) * 128
                ].reshape(C, 16, Z)
        for pair in (2 * xl, 2 * xl + 1):
            spectral = mm(wave_ref[...], iz_ref[pair])
            for g in range(G):
                for h in range(2):
                    channel = 4 * g + 2 * (pair % 2) + h
                    pre = (
                        spectral[g * Y : (g + 1) * Y, h * 128 : (h + 1) * 128]
                        + conv_out[channel]
                        + bias_ref[channel]
                    )
                    delta = cot_ref[0, xl, channel].astype(f32) * gelu_slope(pre)
                    delta_ref[pair, g * Y : (g + 1) * Y, h * 128 : (h + 1) * 128] = delta.astype(bf16)

    analyse(lambda pair: delta_ref[pair], fz_ref, fy_ref, un_ref, modes_ref, step)

    @pl.when(step == XP - 1)
    def _():
        out_ref[...] = modes_ref[...].astype(bf16)


def slab_call(fields, cotangent, mixed, conv, bias, t):
    return pl.pallas_call(
        slab_kernel,
        out_shape=jax.ShapeDtypeStruct((2560, 128), bf16),
        grid=(XP,),
        in_specs=[
            pl.BlockSpec((1, 2, C, Y, Z), lambda i: (0, i, 0, 0, 0)),
            pl.BlockSpec((1, 2, C, Y, Z), lambda i: (0, i, 0, 0, 0)),
            full((2560, 128)),
            full((320, 320)),
            pl.BlockSpec(memory_space=pltpu.SMEM),
            full((256, 128)),
            full((4, 256, 256)),
            full((1, 128)),
            full((4, 256, 256)),
            full((128, 256)),
            full((1, 256)),
        ],
        out_specs=pl.BlockSpec((2560, 128), lambda i: (0, 0)),
        scratch_shapes=[
            pltpu.VMEM((2560, 128), f32),
            pltpu.VMEM((2560, 128), f32),
            pltpu.VMEM((C, Y, Z), f32),
            pltpu.VMEM((640, 256), bf16),
            pltpu.VMEM((4, 640, 256), bf16),
        ],
        compiler_params=pltpu.CompilerParams(
            dimension_semantics=("arbitrary",), vmem_limit_bytes=60 << 20
        ),
        name="slab",
    )(
        fields, cotangent, mixed, conv, bias, t["inverse_y"], t["inverse_z"],
        t["unscale_inverse"], t["forward_z"], t["forward_y"], t["unscale_back"],
    )


def small_call(kernel, name, out_shape, scratch, *args):
    return pl.pallas_call(
        kernel,
        out_shape=out_shape,
        scratch_shapes=scratch,
        compiler_params=pltpu.CompilerParams(vmem_limit_bytes=60 << 20),
        name=name,
    )(*args)


def lower_half():
    return lax.broadcasted_iota(jnp.int32, (64, 128), 1) < 64


def forward_x_kernel(in_ref, fx_ref, out_ref):
    low = lower_half()
    for gk in range(GA):
        cols = []
        for b in range(2):
            row = (2 * gk + b) * 16
            cols.append(jnp.concatenate([in_ref[j * 320 + row : j * 320 + row + 16, :] for j in range(8)], axis=0))
        right = jnp.concatenate(cols, axis=1)
        out = mm(fx_ref[...], jnp.concatenate([right, right], axis=0))
        first = jnp.where(low, out[:64, :128], out[64:, 128:])
        second = jnp.where(low, out[:64, 128:], out[64:, :128])
        res = first + pltpu.roll(second, 64, 1)
        for r in range(4):
            out_ref[pl.ds(r * GA + gk, 16, stride=40), :] = res[r * 16 : (r + 1) * 16]


def inverse_x_kernel(in_ref, ix_ref, out_ref, wide_ref):
    wide_ref[...] = in_ref[...].astype(f32)
    low = lax.broadcasted_iota(jnp.int32, (128, 128), 1) < 64
    for gk in range(GA):
        rows = [wide_ref[pl.ds(r * GA + gk, 16, stride=40), :] for r in range(4)]
        part = jnp.concatenate(rows, axis=0).astype(bf16)
        out = mm(ix_ref[...], jnp.concatenate([part, part], axis=0))
        first = jnp.where(low, out[:128], pltpu.roll(out[128:], 64, 1)).astype(bf16)
        second = jnp.where(low, pltpu.roll(out[:128], 64, 1), out[128:]).astype(bf16)
        for b, value in enumerate((first, second)):
            row = (2 * gk + b) * 16
            for j in range(8):
                out_ref[j * 320 + row : j * 320 + row + 16, :] = value[j * 16 : (j + 1) * 16]


def weight_kernel(w_ref, place_ref, out_ref, wide_ref):
    wide_ref[...] = w_ref[...].astype(f32)
    cols = [wide_ref[pl.ds(o, 400, stride=4), :].astype(bf16) for o in range(4)]
    out = mm(jnp.concatenate(cols, axis=1), place_ref[...])
    out_ref[0] = out[:, :128]
    out_ref[1] = out[:, 128:]


def spread_channels(in_ref, spread_ref, wide_ref):
    for r in range(40):
        rows = in_ref[pl.ds(r, 16, stride=40), :]
        upper = rows.astype(bf16)
        lower = (rows - upper.astype(f32)).astype(bf16)
        wide_ref[r * 16 : (r + 1) * 16, :] = jnp.concatenate([upper, lower], axis=1)


def mix_kernel(in_ref, spread_ref, w_ref, out_ref, wide_ref, chan_ref, mixed_ref):
    spread_channels(in_ref, spread_ref, wide_ref)
    chan_ref[...] = mm(wide_ref[...], spread_ref[...])
    for kxl in range(2):
        for kya in range(2):
            real = [jnp.zeros((16, 128), f32) for _ in range(G)]
            imag = [jnp.zeros((16, 128), f32) for _ in range(G)]
            for c in range(C):
                row = (kxl * 20 + (c // 4) * 2 + kya) * 16
                lanes = (c % 4) * 128
                s_re = chan_ref[row : row + 16, lanes : lanes + 128]
                s_im = chan_ref[row + 160 : row + 176, lanes : lanes + 128]
                for go in range(G):
                    line = kxl * 200 + c * G + go
                    w_re = w_ref[kya, line : line + 1, :]
                    w_im = w_ref[kya, line + 100 : line + 101, :]
                    real[go] = real[go] + (s_re * w_re - s_im * w_im)
                    imag[go] = imag[go] + (s_re * w_im + s_im * w_re)
            for go in range(G):
                row = kxl * 20 + go * 2 + kya
                mixed_ref[pl.ds(row, 16, stride=40), :] = real[go]
                mixed_ref[pl.ds(row + 10, 16, stride=40), :] = imag[go]
    out_ref[...] = mixed_ref[...].astype(bf16)


def grad_kernel(s_ref, b_ref, spread_ref, out_ref, wide_ref, chan_ref):
    spread_channels(s_ref, spread_ref, wide_ref)
    chan_ref[...] = mm(wide_ref[...], spread_ref[...])
    for kxl in range(2):
        for kya in range(2):
            b_re = [b_ref[pl.ds(kxl * 20 + g * 2 + kya, 16, stride=40), :] for g in range(G)]
            b_im = [b_ref[pl.ds(kxl * 20 + g * 2 + kya + 10, 16, stride=40), :] for g in range(G)]
            for c in range(C):
                row = (kxl * 20 + (c // 4) * 2 + kya) * 16
                lanes = (c % 4) * 128
                s_re = chan_ref[row : row + 16, lanes : lanes + 128]
                s_im = chan_ref[row + 160 : row + 176, lanes : lanes + 128]
                for go in range(G):
                    line = kxl * 200 + c * G + go
                    real = s_re * b_re[go] + s_im * b_im[go]
                    imag = s_re * b_im[go] - s_im * b_re[go]
                    out_ref[kya, line : line + 1, :] = jnp.sum(real, axis=0, keepdims=True)
                    out_ref[kya, line + 100 : line + 101, :] = jnp.sum(imag, axis=0, keepdims=True)


def exchange(values, axis, count):
    blocks = values.reshape(count, -1, 128)
    return lax.all_to_all(blocks, axis, split_axis=0, concat_axis=0, tiled=True).reshape(-1, 128)


def shards(fields, cotangent, spectral_weight, conv_weight, conv_bias):
    t = {name: jnp.asarray(value) for name, value in tables().items()}
    conv = (
        conv_weight.T[:, None, :, None] * jnp.eye(16, dtype=bf16)[None, :, None, :]
    ).reshape(320, 320)

    def to_kx(modes):
        moved = exchange(modes, "mp", MP)
        part = small_call(
            forward_x_kernel, "forward_x", jax.ShapeDtypeStruct((640, 128), f32), [], moved, t["forward_x"]
        )
        return exchange(part, "dp", DP)

    weights = small_call(
        weight_kernel, "weights", jax.ShapeDtypeStruct((2, 400, 128), f32),
        [pltpu.VMEM((1600, 64), f32)], spectral_weight.reshape(1600, 64), t["place"],
    )
    spectra = to_kx(analyse_call(fields, t))
    mixed = small_call(
        mix_kernel, "mix", jax.ShapeDtypeStruct((640, 128), bf16),
        [pltpu.VMEM((640, 256), bf16), pltpu.VMEM((640, 512), f32), pltpu.VMEM((640, 128), f32)],
        spectra, t["spread"], weights,
    )
    slabs = small_call(
        inverse_x_kernel, "inverse_x", jax.ShapeDtypeStruct((2560, 128), bf16),
        [pltpu.VMEM((640, 128), f32)], exchange(mixed, "dp", DP), t["inverse_x"],
    )
    back_modes = slab_call(fields, cotangent, exchange(slabs, "mp", MP), conv, conv_bias, t)
    back = to_kx(back_modes)
    grad = small_call(
        grad_kernel, "grad", jax.ShapeDtypeStruct((2, 400, 128), f32),
        [pltpu.VMEM((640, 256), bf16), pltpu.VMEM((640, 512), f32)], spectra, back, t["spread"],
    )
    grad = grad.reshape(2, 2, 2, C, G, 2, 4, KZ)
    return jnp.transpose(grad, (1, 2, 3, 4, 6, 0, 5, 7)).reshape(2, 2, C, C, 64)


def solution(mesh):
    return jax.shard_map(
        shards,
        mesh=mesh,
        in_specs=(
            P("dp", "mp", None, None, None),
            P("dp", "mp", None, None, None),
            P("dp", None, None, None, "mp"),
            P(),
            P(),
        ),
        out_specs=P("dp", None, None, None, "mp"),
        check_vma=False,
    )
```

```python
import functools

import jax
import jax.numpy as jnp
import ml_dtypes
import numpy as np
from jax import lax
from jax.experimental import pallas as pl
from jax.experimental.pallas import tpu as pltpu
from jax.sharding import PartitionSpec as P

X = 128
Y = 128
Z = 128
C = 20
KX = 32
KY = 32
KZ = 16
DP = 16
MP = 8
XP = 8
G = 5
GK = 20
GA = 10
SUB = 2

bf16 = jnp.bfloat16
f32 = jnp.float32
np_bf16 = ml_dtypes.bfloat16

INV_ROOT_TWO = 0.7071067811865476
TWO_OVER_ROOT_PI = 1.1283791670955126
LOG2_E = 1.4426950408889634


def kept(count, length):
    return np.concatenate([np.arange(count // 2), np.arange(length - count // 2, length)])


def angles(modes, length):
    return 2.0 * np.pi / length * ((modes[:, None] * np.arange(length)[None, :]) % length)


def hi_lo(table):
    upper = table.astype(np_bf16)
    lower = (table - upper.astype(np.float64)).astype(np_bf16)
    return upper, lower


def z_scales():
    candidates = 1.0 + np.arange(512) / 512
    scales = []
    for row in angles(np.arange(KZ), Z):
        values = np.concatenate([np.cos(row), np.sin(row)])[None, :] * candidates[:, None]
        off = ((values.astype(np_bf16).astype(np.float64) - values) ** 2).sum(1) / (values**2).sum(1)
        scales.append(candidates[int(np.argmin(off))])
    return np.array(scales)


@functools.cache
def tables():
    scale = z_scales()
    weight = np.where(np.arange(KZ) == 0, 1.0, 2.0) / (X * Y * Z)
    phase_z = angles(np.arange(KZ), Z)
    cos_z, sin_z = np.cos(phase_z), np.sin(phase_z)
    forward_z = np.zeros((8, Z, 2, 8, KZ))
    inverse_z = np.zeros((4, 2, 8, KZ, 2, Z))
    for q in range(8):
        forward_z[q, :, 0, q, :] = (cos_z * scale[:, None]).T
        forward_z[q, :, 1, q, :] = (sin_z * scale[:, None]).T
        inverse_z[q // 2, 0, q, :, q % 2, :] = cos_z * scale[:, None]
        inverse_z[q // 2, 1, q, :, q % 2, :] = -sin_z * scale[:, None]
    unscale = np.tile(1.0 / scale, 16)[None, :]
    unscale_back = np.tile(0.5 * weight / scale, 16)[None, :]
    unscale_inverse = np.tile(INV_ROOT_TWO * weight / scale, 8)[None, :]
    phase_y = angles(kept(KY, Y), Y)
    cos_y, sin_y = np.cos(phase_y), np.sin(phase_y)
    forward_y = np.zeros((KY, 2, 2, Y))
    forward_y[:, 0, 0], forward_y[:, 0, 1] = cos_y, -sin_y
    forward_y[:, 1, 0], forward_y[:, 1, 1] = -sin_y, -cos_y
    forward_y = np.concatenate(hi_lo(forward_y.reshape(64, 256)), axis=0)
    inverse_y = np.zeros((2, Y, KY, 2))
    inverse_y[0, :, :, 0], inverse_y[0, :, :, 1] = cos_y.T, -sin_y.T
    inverse_y[1, :, :, 0], inverse_y[1, :, :, 1] = sin_y.T, cos_y.T
    inverse_y = np.concatenate(hi_lo(inverse_y.reshape(256, 64)), axis=1)
    phase_x = angles(kept(KX, X), X).reshape(16, 2, 8, 8, 2)
    cos_x, sin_x = np.cos(phase_x), np.sin(phase_x)
    forward_x = np.zeros((2, 2, 2, 16, 8, 2, 8))
    inverse_x = np.zeros((2, 8, 2, 8, 2, 2, 16))
    cos_f = np.transpose(cos_x, (4, 1, 0, 2, 3))
    sin_f = np.transpose(sin_x, (4, 1, 0, 2, 3))
    forward_x[:, :, 0, :, :, 0, :] = cos_f
    forward_x[:, :, 0, :, :, 1, :] = sin_f
    forward_x[:, :, 1, :, :, 0, :] = -sin_f
    forward_x[:, :, 1, :, :, 1, :] = cos_f
    cos_i = np.transpose(cos_x, (4, 2, 3, 1, 0))
    sin_i = np.transpose(sin_x, (4, 2, 3, 1, 0))
    inverse_x[:, :, 0, :, :, 0, :] = cos_i
    inverse_x[:, :, 0, :, :, 1, :] = -sin_i
    inverse_x[:, :, 1, :, :, 0, :] = sin_i
    inverse_x[:, :, 1, :, :, 1, :] = cos_i
    forward_x = np.concatenate(hi_lo(forward_x.reshape(128, 128)), axis=1)
    inverse_x = np.concatenate(hi_lo(inverse_x.reshape(256, 64)), axis=1)
    spread = np.zeros((2, 4, KZ, 4, 2, 4, KZ))
    for channel in range(4):
        for place in range(4):
            for b in range(2):
                spread[b, channel, np.arange(KZ), channel, b, place, np.arange(KZ)] = 1.0
    spread = spread.reshape(128, 512)
    place = np.zeros((4, 4, KZ, 2, 2, 4, KZ))
    for o in range(4):
        for kyl in range(4):
            place[o, kyl, np.arange(KZ), kyl // 2, kyl % 2, o, np.arange(KZ)] = 1.0
    gather = np.zeros((2, 2, 4, KZ, 4, 2, 2, 2, KZ))
    for o in range(4):
        for a in range(2):
            for b in range(2):
                gather[a, b, o, np.arange(KZ), o, 0, a, b, np.arange(KZ)] = 1.0
    gather = gather.reshape(256, 512)
    return dict(
        gather=np.concatenate([gather, gather], axis=0).astype(np_bf16),
        forward_z=forward_z.reshape(4, 256, 256).astype(np_bf16),
        inverse_z=inverse_z.reshape(4, 256, 256).astype(np_bf16),
        unscale=unscale.astype(np.float32),
        unscale_back=unscale_back.astype(np.float32),
        unscale_inverse=unscale_inverse.astype(np.float32),
        forward_y=forward_y,
        inverse_y=inverse_y,
        forward_x=forward_x,
        inverse_x=inverse_x,
        spread=spread.astype(np_bf16),
        place=place.reshape(256, 256).astype(np_bf16),
    )


def mm(a, b):
    return jnp.dot(a, b, preferred_element_type=f32)


def z_transform(lhs_of, fz_ref, un_ref, groups):
    total = mm(lhs_of(0, groups), fz_ref[0])
    for pair in range(1, 4):
        total = total + mm(lhs_of(pair, groups), fz_ref[pair])
    return total * un_ref[...]


def y_transform(part, fy_ref, modes_ref, g, at):
    both = jnp.concatenate([part[:, :128], part[:, 128:]], axis=0)
    upper = both.astype(bf16)
    lower = (both - upper.astype(f32)).astype(bf16)
    out = mm(fy_ref[...], jnp.concatenate([upper, lower], axis=1))
    modes = out[:64, :128] + out[64:, :128] + out[:64, 128:]
    for j in range(MP):
        modes_ref[pl.ds(j * 320 + g * 64 + at, 8, stride=8), :] = modes[j * 8 : (j + 1) * 8]


def analyse(lhs_of, fz_ref, fy_ref, un_ref, modes_ref, at, groups):
    total = z_transform(lhs_of, fz_ref, un_ref, groups)
    for k, g in enumerate(groups):
        y_transform(total[k * Y : (k + 1) * Y], fy_ref, modes_ref, g, at)


HALVES = ((0, 1, 2), (3, 4))


def analyse_kernel(*refs):
    field_refs, (fz_ref, fy_ref, un_ref, out_ref, modes_ref) = refs[: 2 * SUB], refs[2 * SUB :]
    step = pl.program_id(0)

    for sub in range(SUB):

        def lhs(pair, groups, sub=sub):
            xl, c4 = 2 * sub + pair // 2, 2 * (pair % 2)
            rows = [
                jnp.concatenate(
                    [field_refs[xl][0, 0, 4 * g + c4], field_refs[xl][0, 0, 4 * g + c4 + 1]], axis=1
                )
                for g in groups
            ]
            return jnp.concatenate(rows, axis=0)

        totals = [z_transform(lhs, fz_ref, un_ref, groups) for groups in HALVES]
        for total, groups in zip(totals, HALVES):
            for k, g in enumerate(groups):
                y_transform(total[k * Y : (k + 1) * Y], fy_ref, modes_ref, g, step * SUB + sub)

    @pl.when(step == XP // SUB - 1)
    def _():
        out_ref[...] = modes_ref[...].astype(bf16)


def x_streams():
    return [
        pl.BlockSpec((1, 1, C, Y, Z), lambda i, k=k: (0, 2 * SUB * i + k, 0, 0, 0))
        for k in range(2 * SUB)
    ]


def full(shape):
    zeros = (0,) * len(shape)
    return pl.BlockSpec(shape, lambda *_: zeros, pipeline_mode=pl.Buffered(1))


def analyse_call(fields, t):
    return pl.pallas_call(
        analyse_kernel,
        out_shape=jax.ShapeDtypeStruct((2560, 128), bf16),
        grid=(XP // SUB,),
        in_specs=[
            *x_streams(),
            full((4, 256, 256)),
            full((128, 256)),
            full((1, 256)),
        ],
        out_specs=pl.BlockSpec((2560, 128), lambda i: (0, 0)),
        scratch_shapes=[pltpu.VMEM((2560, 128), f32)],
        compiler_params=pltpu.CompilerParams(
            dimension_semantics=("arbitrary",), vmem_limit_bytes=54 << 20
        ),
        name="analyse",
    )(*[fields] * (2 * SUB), t["forward_z"], t["forward_y"], t["unscale"])


def conv_kernel(*refs):
    field_refs, (conv_ref, bias_ref), out_refs = refs[: 2 * SUB], refs[2 * SUB : -2 * SUB], refs[-2 * SUB :]
    bias = jnp.concatenate([bias_ref[...], bias_ref[...]], axis=1)
    for xl in range(2 * SUB):
        for yp in range(4):
            right = jnp.concatenate(
                [
                    field_refs[xl][0, 0, :, yp * 32 + h * 16 : yp * 32 + (h + 1) * 16, :].reshape(320, Z)
                    for h in range(2)
                ],
                axis=1,
            )
            out = ((mm(conv_ref[...], right) + bias) * INV_ROOT_TWO).astype(bf16)
            for h in range(2):
                out_refs[xl][0, :, yp * 32 + h * 16 : yp * 32 + (h + 1) * 16, :] = out[
                    :, h * 128 : (h + 1) * 128
                ].reshape(C, 16, Z)


def conv_call(fields, conv, bias):
    return pl.pallas_call(
        conv_kernel,
        out_shape=[jax.ShapeDtypeStruct((XP // SUB, C, Y, Z), bf16)] * (2 * SUB),
        grid=(XP // SUB,),
        in_specs=[
            *x_streams(),
            full((320, 320)),
            full((320, 128)),
        ],
        out_specs=[pl.BlockSpec((1, C, Y, Z), lambda i: (i, 0, 0, 0))] * (2 * SUB),
        compiler_params=pltpu.CompilerParams(
            dimension_semantics=("arbitrary",), vmem_limit_bytes=54 << 20
        ),
        cost_estimate=pl.CostEstimate(
            flops=2 * 16 * Y * Z * 320 * C, bytes_accessed=4 * 16 * C * Y * Z, transcendentals=0
        ),
        name="conv",
    )(*[fields] * (2 * SUB), conv, bias)


def slab_kernel(*refs):
    conv_refs, cot_refs = refs[: 2 * SUB], refs[2 * SUB : 4 * SUB]
    mixed_ref, iy_ref, iz_ref, uni_ref, fz_ref, fy_ref, un_ref, out_ref = refs[4 * SUB : 4 * SUB + 8]
    modes_ref, mixed_f32, wave_ref, delta_ref = refs[4 * SUB + 8 :]
    step = pl.program_id(0)

    def wave(at, slot, g):
        rows = [mixed_f32[pl.ds(j * 320 + g * 64 + at, 8, stride=8), :] for j in range(MP)]
        part = jnp.concatenate(rows, axis=0).astype(bf16)
        out = mm(iy_ref[...], jnp.concatenate([part, part], axis=0))
        out = (out * uni_ref[...]).astype(bf16)
        wave_ref[slot, g * Y : (g + 1) * Y, :128] = out[:Y]
        wave_ref[slot, g * Y : (g + 1) * Y, 128:] = out[Y:]

    def delta(sub, pair, spectral):
        xl = 2 * sub + pair // 2
        for g in range(G):
            for h in range(2):
                channel = 4 * g + 2 * (pair % 2) + h
                u = spectral[g * Y : (g + 1) * Y, h * 128 : (h + 1) * 128] + conv_refs[xl][
                    0, channel
                ].astype(f32)
                bell = jnp.exp2(u * u * -LOG2_E)
                slope = 1.0 + (lax.erf(u) + (u * TWO_OVER_ROOT_PI) * bell)
                value = cot_refs[xl][0, 0, channel].astype(f32) * slope
                delta_ref[sub % 2, pair, g * Y : (g + 1) * Y, h * 128 : (h + 1) * 128] = value.astype(bf16)

    def lhs_of(slot):
        return lambda pair, groups: delta_ref[slot, pair, groups[0] * Y : (groups[-1] + 1) * Y, :]

    @pl.when(step == 0)
    def _():
        mixed_f32[...] = mixed_ref[...].astype(f32)
        for g in range(G):
            wave(0, 0, g)

    for sub in range(SUB):
        at = step * SUB + sub
        before = jnp.maximum(at - 1, 0)
        after = jnp.minimum(at + 1, XP - 1)
        slot = sub % 2
        lhs = lhs_of(1 - slot)
        spectral = [mm(wave_ref[slot], iz_ref[0])]
        totals = []
        for pair in range(4):
            if pair < 3:
                spectral.append(mm(wave_ref[slot], iz_ref[pair + 1]))
            delta(sub, pair, spectral[pair])
            if pair < 2:
                totals.append(z_transform(lhs, fz_ref, un_ref, HALVES[pair]))
            else:
                for k, g in enumerate(HALVES[pair - 2]):
                    y_transform(totals[pair - 2][k * Y : (k + 1) * Y], fy_ref, modes_ref, g, before)
            for g in ((0, 1), (2,), (3,), (4,))[pair]:
                wave(after, 1 - slot, g)

    @pl.when(step == XP // SUB - 1)
    def _():
        lhs = lhs_of((SUB - 1) % 2)
        for groups in HALVES:
            analyse(lhs, fz_ref, fy_ref, un_ref, modes_ref, XP - 1, groups)
        out_ref[...] = modes_ref[...].astype(bf16)


def slab_call(conv, cotangent, mixed, t):
    return pl.pallas_call(
        slab_kernel,
        out_shape=jax.ShapeDtypeStruct((2560, 128), bf16),
        grid=(XP // SUB,),
        in_specs=[
            *[pl.BlockSpec((1, C, Y, Z), lambda i: (i, 0, 0, 0))] * (2 * SUB),
            *x_streams(),
            full((2560, 128)),
            full((256, 128)),
            full((4, 256, 256)),
            full((1, 128)),
            full((4, 256, 256)),
            full((128, 256)),
            full((1, 256)),
        ],
        out_specs=pl.BlockSpec((2560, 128), lambda i: (0, 0)),
        scratch_shapes=[
            pltpu.VMEM((2560, 128), f32),
            pltpu.VMEM((2560, 128), f32),
            pltpu.VMEM((SUB, 640, 256), bf16),
            pltpu.VMEM((SUB, 4, 640, 256), bf16),
        ],
        compiler_params=pltpu.CompilerParams(
            dimension_semantics=("arbitrary",), vmem_limit_bytes=54 << 20
        ),
        name="slab",
    )(
        *conv, *[cotangent] * (2 * SUB), mixed, t["inverse_y"], t["inverse_z"],
        t["unscale_inverse"], t["forward_z"], t["forward_y"], t["unscale_back"],
    )


def small_call(kernel, name, out_shape, scratch, *args):
    return pl.pallas_call(
        kernel,
        out_shape=out_shape,
        scratch_shapes=scratch,
        compiler_params=pltpu.CompilerParams(vmem_limit_bytes=10 << 20),
        name=name,
    )(*args)


def lower_half():
    return lax.broadcasted_iota(jnp.int32, (64, 128), 1) < 64


def forward_x_kernel(in_ref, fx_ref, out_ref, wide_ref):
    low = lower_half()
    for gk in range(GA):
        cols = []
        for b in range(2):
            row = (2 * gk + b) * 16
            cols.append(jnp.concatenate([in_ref[j * 320 + row : j * 320 + row + 16, :] for j in range(8)], axis=0))
        right = jnp.concatenate(cols, axis=1)
        out = mm(fx_ref[...], jnp.concatenate([right, right], axis=0))
        first = jnp.where(low, out[:64, :128], out[64:, 128:])
        second = jnp.where(low, out[:64, 128:], out[64:, :128])
        res = first + pltpu.roll(second, 64, 1)
        for r in range(4):
            wide_ref[pl.ds(r * GA + gk, 16, stride=40), :] = res[r * 16 : (r + 1) * 16]
    out_ref[...] = wide_ref[...].astype(bf16)


def inverse_x_kernel(in_ref, ix_ref, out_ref, wide_ref):
    wide_ref[...] = in_ref[...].astype(f32)
    low = lax.broadcasted_iota(jnp.int32, (128, 128), 1) < 64
    for gk in range(GA):
        rows = [wide_ref[pl.ds(r * GA + gk, 16, stride=40), :] for r in range(4)]
        part = jnp.concatenate(rows, axis=0).astype(bf16)
        out = mm(ix_ref[...], jnp.concatenate([part, part], axis=0))
        first = jnp.where(low, out[:128], pltpu.roll(out[128:], 64, 1)).astype(bf16)
        second = jnp.where(low, pltpu.roll(out[:128], 64, 1), out[128:]).astype(bf16)
        for b, value in enumerate((first, second)):
            row = (2 * gk + b) * 16
            for j in range(8):
                out_ref[j * 320 + row : j * 320 + row + 16, :] = value[j * 16 : (j + 1) * 16]


def weight_kernel(w_ref, place_ref, out_ref, wide_ref):
    wide_ref[...] = w_ref[...].astype(f32)
    cols = [wide_ref[pl.ds(o, 400, stride=4), :].astype(bf16) for o in range(4)]
    out = mm(jnp.concatenate(cols, axis=1), place_ref[...])
    out_ref[0] = out[:, :128]
    out_ref[1] = out[:, 128:]


def spread_channels(in_ref, spread_ref, wide_ref, rows_ref, chan_ref):
    wide_ref[...] = in_ref[...].astype(f32)
    for r in range(40):
        rows_ref[r * 16 : (r + 1) * 16, :] = wide_ref[pl.ds(r, 16, stride=40), :].astype(bf16)
    chan_ref[...] = mm(rows_ref[...], spread_ref[...])


def channel_parts(chan_ref, kxl, kya, c):
    row = (kxl * 20 + (c // 4) * 2 + kya) * 16
    lanes = (c % 4) * 128
    return (
        chan_ref[row : row + 16, lanes : lanes + 128],
        chan_ref[row + 160 : row + 176, lanes : lanes + 128],
    )


SPREAD_SCRATCH = (
    pltpu.VMEM((640, 128), f32), pltpu.VMEM((640, 128), bf16), pltpu.VMEM((640, 512), f32)
)


def mix_kernel(in_ref, spread_ref, w_ref, out_ref, wide_ref, rows_ref, chan_ref):
    spread_channels(in_ref, spread_ref, wide_ref, rows_ref, chan_ref)
    for kxl in range(2):
        for kya in range(2):
            real = [jnp.zeros((16, 128), f32) for _ in range(G)]
            imag = [jnp.zeros((16, 128), f32) for _ in range(G)]
            for c in range(C):
                s_re, s_im = channel_parts(chan_ref, kxl, kya, c)
                for go in range(G):
                    line = kxl * 200 + c * G + go
                    w_re = w_ref[kya, line : line + 1, :]
                    w_im = w_ref[kya, line + 100 : line + 101, :]
                    real[go] = real[go] + (s_re * w_re - s_im * w_im)
                    imag[go] = imag[go] + (s_re * w_im + s_im * w_re)
            for go in range(G):
                row = kxl * 20 + go * 2 + kya
                wide_ref[pl.ds(row, 16, stride=40), :] = real[go]
                wide_ref[pl.ds(row + 10, 16, stride=40), :] = imag[go]
    out_ref[...] = wide_ref[...].astype(bf16)


def grad_kernel(s_ref, b_ref, spread_ref, gather_ref, out_ref, wide_ref, rows_ref, chan_ref, sum_ref):
    spread_channels(s_ref, spread_ref, wide_ref, rows_ref, chan_ref)
    wide_ref[...] = b_ref[...].astype(f32)
    for kxl in range(2):
        for kya in range(2):
            b_re = [wide_ref[pl.ds(kxl * 20 + g * 2 + kya, 16, stride=40), :] for g in range(G)]
            b_im = [wide_ref[pl.ds(kxl * 20 + g * 2 + kya + 10, 16, stride=40), :] for g in range(G)]
            for c in range(C):
                s_re, s_im = channel_parts(chan_ref, kxl, kya, c)
                for go in range(G):
                    line = kxl * 100 + c * G + go
                    real = s_re * b_re[go] + s_im * b_im[go]
                    imag = s_re * b_im[go] - s_im * b_re[go]
                    lanes = slice(kya * 128, kya * 128 + 128)
                    sum_ref[line : line + 1, lanes] = jnp.sum(real, axis=0, keepdims=True)
                    sum_ref[200 + line : 201 + line, lanes] = jnp.sum(imag, axis=0, keepdims=True)
    sums = sum_ref[...]
    upper = sums.astype(bf16)
    lower = (sums - upper.astype(f32)).astype(bf16)
    placed = mm(jnp.concatenate([upper, lower], axis=1), gather_ref[...])
    for o in range(4):
        for part in range(2):
            out_ref[pl.ds(o * 2 + part, 200, stride=8), :] = placed[
                part * 200 : (part + 1) * 200, o * 128 : o * 128 + 128
            ]


def exchange(values, axis, count):
    blocks = values.reshape(count, -1, 128)
    return lax.all_to_all(blocks, axis, split_axis=0, concat_axis=0, tiled=True).reshape(-1, 128)


def shards(fields, cotangent, spectral_weight, conv_weight, conv_bias):
    t = {name: jnp.asarray(value) for name, value in tables().items()}
    conv = (
        conv_weight.T[:, None, :, None] * jnp.eye(16, dtype=bf16)[None, :, None, :]
    ).reshape(320, 320)

    bias = jnp.broadcast_to(conv_bias[:, None, None], (C, 16, 128)).reshape(320, 128)

    def to_kx(modes):
        moved = exchange(modes, "mp", MP)
        part = small_call(
            forward_x_kernel, "forward_x", jax.ShapeDtypeStruct((640, 128), bf16),
            [pltpu.VMEM((640, 128), f32)], moved, t["forward_x"],
        )
        return exchange(part, "dp", DP)

    weights = small_call(
        weight_kernel, "weights", jax.ShapeDtypeStruct((2, 400, 128), f32),
        [pltpu.VMEM((1600, 64), f32)], spectral_weight.reshape(1600, 64), t["place"],
    )
    spectra = to_kx(analyse_call(fields, t))
    mixed = small_call(
        mix_kernel, "mix", jax.ShapeDtypeStruct((640, 128), bf16), SPREAD_SCRATCH,
        spectra, t["spread"], weights,
    )
    slabs = small_call(
        inverse_x_kernel, "inverse_x", jax.ShapeDtypeStruct((2560, 128), bf16),
        [pltpu.VMEM((640, 128), f32)], exchange(mixed, "dp", DP), t["inverse_x"],
    )
    slabs, conv = lax.optimization_barrier((slabs, conv))
    conv_term = conv_call(fields, conv, bias)
    back = to_kx(slab_call(conv_term, cotangent, exchange(slabs, "mp", MP), t))
    grad = small_call(
        grad_kernel, "grad", jax.ShapeDtypeStruct((1600, 128), f32),
        (*SPREAD_SCRATCH, pltpu.VMEM((400, 256), f32)), spectra, back, t["spread"], t["gather"],
    )
    return jnp.transpose(grad.reshape(2, C, C, 2, 128)[..., :64], (0, 3, 1, 2, 4))


def solution(mesh):
    return jax.shard_map(
        shards,
        mesh=mesh,
        in_specs=(
            P("dp", "mp", None, None, None),
            P("dp", "mp", None, None, None),
            P("dp", None, None, None, "mp"),
            P(),
            P(),
        ),
        out_specs=P("dp", None, None, None, "mp"),
        check_vma=False,
    )
```

```python
import functools

import jax
import jax.numpy as jnp
import ml_dtypes
import numpy as np
from jax import lax
from jax.experimental import pallas as pl
from jax.experimental.pallas import tpu as pltpu
from jax.sharding import PartitionSpec as P

X = 128
Y = 128
Z = 128
C = 20
KX = 32
KY = 32
KZ = 16
DP = 16
MP = 8
XP = 8
G = 5
GK = 20
GA = 10
SUB = 2

bf16 = jnp.bfloat16
f32 = jnp.float32
np_bf16 = ml_dtypes.bfloat16

INV_ROOT_TWO = 0.7071067811865476
TWO_OVER_ROOT_PI = 1.1283791670955126
LOG2_E = 1.4426950408889634


def kept(count, length):
    return np.concatenate([np.arange(count // 2), np.arange(length - count // 2, length)])


def angles(modes, length):
    return 2.0 * np.pi / length * ((modes[:, None] * np.arange(length)[None, :]) % length)


def hi_lo(table):
    upper = table.astype(np_bf16)
    lower = (table - upper.astype(np.float64)).astype(np_bf16)
    return upper, lower


def z_scales():
    candidates = 1.0 + np.arange(512) / 512
    scales = []
    for row in angles(np.arange(KZ), Z):
        values = np.concatenate([np.cos(row), np.sin(row)])[None, :] * candidates[:, None]
        off = ((values.astype(np_bf16).astype(np.float64) - values) ** 2).sum(1) / (values**2).sum(1)
        scales.append(candidates[int(np.argmin(off))])
    return np.array(scales)


@functools.cache
def tables():
    scale = z_scales()
    weight = np.where(np.arange(KZ) == 0, 1.0, 2.0) / (X * Y * Z)
    phase_z = angles(np.arange(KZ), Z)
    cos_z, sin_z = np.cos(phase_z), np.sin(phase_z)
    forward_z = np.zeros((8, Z, 2, 8, KZ))
    inverse_z = np.zeros((4, 2, 8, KZ, 2, Z))
    for q in range(8):
        forward_z[q, :, 0, q, :] = (cos_z * scale[:, None]).T
        forward_z[q, :, 1, q, :] = (sin_z * scale[:, None]).T
        inverse_z[q // 2, 0, q, :, q % 2, :] = cos_z * scale[:, None]
        inverse_z[q // 2, 1, q, :, q % 2, :] = -sin_z * scale[:, None]
    unscale = np.tile(1.0 / scale, 16)[None, :]
    unscale_back = np.tile(0.5 * weight / scale, 16)[None, :]
    unscale_inverse = np.tile(INV_ROOT_TWO * weight / scale, 8)[None, :]
    phase_y = angles(kept(KY, Y), Y)
    cos_y, sin_y = np.cos(phase_y), np.sin(phase_y)
    forward_y = np.zeros((KY, 2, 2, Y))
    forward_y[:, 0, 0], forward_y[:, 0, 1] = cos_y, -sin_y
    forward_y[:, 1, 0], forward_y[:, 1, 1] = -sin_y, -cos_y
    forward_y = np.concatenate(hi_lo(forward_y.reshape(64, 256)), axis=0)
    inverse_y = np.zeros((2, Y, KY, 2))
    inverse_y[0, :, :, 0], inverse_y[0, :, :, 1] = cos_y.T, -sin_y.T
    inverse_y[1, :, :, 0], inverse_y[1, :, :, 1] = sin_y.T, cos_y.T
    inverse_y = np.concatenate(hi_lo(inverse_y.reshape(256, 64)), axis=1)
    phase_x = angles(kept(KX, X), X).reshape(16, 2, 8, 8, 2)
    cos_x, sin_x = np.cos(phase_x), np.sin(phase_x)
    forward_x = np.zeros((2, 2, 2, 16, 8, 2, 8))
    inverse_x = np.zeros((2, 8, 2, 8, 2, 2, 16))
    cos_f = np.transpose(cos_x, (4, 1, 0, 2, 3))
    sin_f = np.transpose(sin_x, (4, 1, 0, 2, 3))
    forward_x[:, :, 0, :, :, 0, :] = cos_f
    forward_x[:, :, 0, :, :, 1, :] = sin_f
    forward_x[:, :, 1, :, :, 0, :] = -sin_f
    forward_x[:, :, 1, :, :, 1, :] = cos_f
    cos_i = np.transpose(cos_x, (4, 2, 3, 1, 0))
    sin_i = np.transpose(sin_x, (4, 2, 3, 1, 0))
    inverse_x[:, :, 0, :, :, 0, :] = cos_i
    inverse_x[:, :, 0, :, :, 1, :] = -sin_i
    inverse_x[:, :, 1, :, :, 0, :] = sin_i
    inverse_x[:, :, 1, :, :, 1, :] = cos_i
    forward_x = np.concatenate(hi_lo(forward_x.reshape(128, 128)), axis=1)
    inverse_x = np.concatenate(hi_lo(inverse_x.reshape(256, 64)), axis=1)
    spread = np.zeros((2, 4, KZ, 4, 2, 4, KZ))
    for channel in range(4):
        for place in range(4):
            for b in range(2):
                spread[b, channel, np.arange(KZ), channel, b, place, np.arange(KZ)] = 1.0
    spread = spread.reshape(128, 512)
    place = np.zeros((4, 4, KZ, 2, 2, 4, KZ))
    for o in range(4):
        for kyl in range(4):
            place[o, kyl, np.arange(KZ), kyl // 2, kyl % 2, o, np.arange(KZ)] = 1.0
    gather = np.zeros((2, 2, 4, KZ, 4, 2, 2, 2, KZ))
    for o in range(4):
        for a in range(2):
            for b in range(2):
                gather[a, b, o, np.arange(KZ), o, 0, a, b, np.arange(KZ)] = 1.0
    gather = gather.reshape(256, 512)
    return dict(
        gather=np.concatenate([gather, gather], axis=0).astype(np_bf16),
        forward_z=forward_z.reshape(4, 256, 256).astype(np_bf16),
        inverse_z=inverse_z.reshape(4, 256, 256).astype(np_bf16),
        unscale=unscale.astype(np.float32),
        unscale_back=unscale_back.astype(np.float32),
        unscale_inverse=unscale_inverse.astype(np.float32),
        forward_y=forward_y,
        inverse_y=inverse_y,
        forward_x=forward_x,
        inverse_x=inverse_x,
        spread=spread.astype(np_bf16),
        place=place.reshape(256, 256).astype(np_bf16),
    )


def mm(a, b):
    return jnp.dot(a, b, preferred_element_type=f32)


def z_transform(lhs_of, fz_ref, un_ref, groups):
    total = mm(lhs_of(0, groups), fz_ref[0])
    for pair in range(1, 4):
        total = total + mm(lhs_of(pair, groups), fz_ref[pair])
    return total * un_ref[...]


def y_transform(part, fy_ref, modes_ref, g, at):
    both = jnp.concatenate([part[:, :128], part[:, 128:]], axis=0)
    upper = both.astype(bf16)
    lower = (both - upper.astype(f32)).astype(bf16)
    out = mm(fy_ref[...], jnp.concatenate([upper, lower], axis=1))
    modes = out[:64, :128] + out[64:, :128] + out[:64, 128:]
    for j in range(MP):
        modes_ref[pl.ds(j * 320 + g * 64 + at, 8, stride=8), :] = modes[j * 8 : (j + 1) * 8]


def analyse(lhs_of, fz_ref, fy_ref, un_ref, modes_ref, at, groups):
    total = z_transform(lhs_of, fz_ref, un_ref, groups)
    for k, g in enumerate(groups):
        y_transform(total[k * Y : (k + 1) * Y], fy_ref, modes_ref, g, at)


HALVES = ((0, 1, 2), (3, 4))


def analyse_kernel(*refs):
    field_refs, (fz_ref, fy_ref, un_ref, out_ref, modes_ref) = refs[: 2 * SUB], refs[2 * SUB :]
    step = pl.program_id(0)

    def lhs_of(sub):
        def lhs(pair, groups):
            xl, c4 = 2 * sub + pair // 2, 2 * (pair % 2)
            rows = [
                jnp.concatenate(
                    [field_refs[xl][0, 0, 4 * g + c4], field_refs[xl][0, 0, 4 * g + c4 + 1]], axis=1
                )
                for g in groups
            ]
            return jnp.concatenate(rows, axis=0)

        return lhs

    totals = [z_transform(lhs_of(sub), fz_ref, un_ref, range(G)) for sub in range(SUB)]
    for g in range(G):
        for sub in range(SUB):
            y_transform(totals[sub][g * Y : (g + 1) * Y], fy_ref, modes_ref, g, step * SUB + sub)

    @pl.when(step == XP // SUB - 1)
    def _():
        out_ref[...] = modes_ref[...].astype(bf16)


def x_streams():
    return [
        pl.BlockSpec((1, 1, C, Y, Z), lambda i, k=k: (0, 2 * SUB * i + k, 0, 0, 0))
        for k in range(2 * SUB)
    ]


def in_hbm(array):
    return pltpu.with_memory_space_constraint(array, pltpu.HBM)


def full(shape):
    zeros = (0,) * len(shape)
    return pl.BlockSpec(shape, lambda *_: zeros, pipeline_mode=pl.Buffered(1))


def analyse_call(fields, t):
    return pl.pallas_call(
        analyse_kernel,
        out_shape=jax.ShapeDtypeStruct((2560, 128), bf16),
        grid=(XP // SUB,),
        in_specs=[
            *x_streams(),
            full((4, 256, 256)),
            full((128, 256)),
            full((1, 256)),
        ],
        out_specs=pl.BlockSpec((2560, 128), lambda i: (0, 0)),
        scratch_shapes=[pltpu.VMEM((2560, 128), f32)],
        compiler_params=pltpu.CompilerParams(
            dimension_semantics=("arbitrary",), vmem_limit_bytes=44 << 20
        ),
        name="analyse",
    )(*map(in_hbm, [*[fields] * (2 * SUB), t["forward_z"], t["forward_y"], t["unscale"]]))


def conv_kernel(*refs):
    field_refs, (conv_ref, bias_ref), out_refs = refs[: 2 * SUB], refs[2 * SUB : -2 * SUB], refs[-2 * SUB :]
    bias = jnp.concatenate([bias_ref[...], bias_ref[...]], axis=1)
    for xl in range(2 * SUB):
        for yp in range(4):
            right = jnp.concatenate(
                [
                    field_refs[xl][0, 0, :, yp * 32 + h * 16 : yp * 32 + (h + 1) * 16, :].reshape(320, Z)
                    for h in range(2)
                ],
                axis=1,
            )
            out = ((mm(conv_ref[...], right) + bias) * INV_ROOT_TWO).astype(bf16)
            for h in range(2):
                out_refs[xl][0, :, yp * 32 + h * 16 : yp * 32 + (h + 1) * 16, :] = out[
                    :, h * 128 : (h + 1) * 128
                ].reshape(C, 16, Z)


def conv_call(fields, conv, bias):
    return pl.pallas_call(
        conv_kernel,
        out_shape=[pltpu.HBM((XP // SUB, C, Y, Z), bf16)] * (2 * SUB),
        grid=(XP // SUB,),
        in_specs=[
            *x_streams(),
            full((320, 320)),
            full((320, 128)),
        ],
        out_specs=[pl.BlockSpec((1, C, Y, Z), lambda i: (i, 0, 0, 0))] * (2 * SUB),
        compiler_params=pltpu.CompilerParams(
            dimension_semantics=("arbitrary",), vmem_limit_bytes=44 << 20
        ),
        cost_estimate=pl.CostEstimate(
            flops=2 * 16 * Y * Z * 320 * C, bytes_accessed=4 * 16 * C * Y * Z, transcendentals=0
        ),
        name="conv",
    )(*map(in_hbm, [fields] * (2 * SUB)), conv, bias)


def slab_kernel(*refs):
    conv_refs, cot_refs = refs[: 2 * SUB], refs[2 * SUB : 4 * SUB]
    mixed_ref, iy_ref, iz_ref, uni_ref, fz_ref, fy_ref, un_ref, out_ref = refs[4 * SUB : 4 * SUB + 8]
    modes_ref, mixed_f32, wave_ref, delta_ref = refs[4 * SUB + 8 :]
    step = pl.program_id(0)

    def wave(at, slot, g):
        rows = [mixed_f32[pl.ds(j * 320 + g * 64 + at, 8, stride=8), :] for j in range(MP)]
        part = jnp.concatenate(rows, axis=0).astype(bf16)
        out = mm(iy_ref[...], jnp.concatenate([part, part], axis=0))
        out = (out * uni_ref[...]).astype(bf16)
        wave_ref[slot, g * Y : (g + 1) * Y, :128] = out[:Y]
        wave_ref[slot, g * Y : (g + 1) * Y, 128:] = out[Y:]

    def delta(sub, pair, spectral):
        xl = 2 * sub + pair // 2
        for g in range(G):
            for h in range(2):
                channel = 4 * g + 2 * (pair % 2) + h
                u = spectral[g * Y : (g + 1) * Y, h * 128 : (h + 1) * 128] + conv_refs[xl][
                    0, channel
                ].astype(f32)
                bell = jnp.exp2(u * u * -LOG2_E)
                slope = 1.0 + (lax.erf(u) + (u * TWO_OVER_ROOT_PI) * bell)
                value = cot_refs[xl][0, 0, channel].astype(f32) * slope
                delta_ref[sub % 2, pair, g * Y : (g + 1) * Y, h * 128 : (h + 1) * 128] = value.astype(bf16)

    def lhs_of(slot):
        return lambda pair, groups: delta_ref[slot, pair, groups[0] * Y : (groups[-1] + 1) * Y, :]

    @pl.when(step == 0)
    def _():
        mixed_f32[...] = mixed_ref[...].astype(f32)
        for g in range(G):
            wave(0, 0, g)

    for sub in range(SUB):
        at = step * SUB + sub
        before = jnp.maximum(at - 1, 0)
        after = jnp.minimum(at + 1, XP - 1)
        slot = sub % 2
        lhs = lhs_of(1 - slot)
        spectral = [mm(wave_ref[slot], iz_ref[0])]
        totals = []
        for pair in range(4):
            if pair < 3:
                spectral.append(mm(wave_ref[slot], iz_ref[pair + 1]))
            delta(sub, pair, spectral[pair])
            if pair < 2:
                totals.append(z_transform(lhs, fz_ref, un_ref, HALVES[pair]))
            else:
                for k, g in enumerate(HALVES[pair - 2]):
                    y_transform(totals[pair - 2][k * Y : (k + 1) * Y], fy_ref, modes_ref, g, before)
            for g in ((0, 1), (2,), (3,), (4,))[pair]:
                wave(after, 1 - slot, g)

    @pl.when(step == XP // SUB - 1)
    def _():
        lhs = lhs_of((SUB - 1) % 2)
        analyse(lhs, fz_ref, fy_ref, un_ref, modes_ref, XP - 1, range(G))
        out_ref[...] = modes_ref[...].astype(bf16)


def slab_call(conv, cotangent, mixed, t):
    return pl.pallas_call(
        slab_kernel,
        out_shape=jax.ShapeDtypeStruct((2560, 128), bf16),
        grid=(XP // SUB,),
        in_specs=[
            *[pl.BlockSpec((1, C, Y, Z), lambda i: (i, 0, 0, 0))] * (2 * SUB),
            *x_streams(),
            full((2560, 128)),
            full((256, 128)),
            full((4, 256, 256)),
            full((1, 128)),
            full((4, 256, 256)),
            full((128, 256)),
            full((1, 256)),
        ],
        out_specs=pl.BlockSpec((2560, 128), lambda i: (0, 0)),
        scratch_shapes=[
            pltpu.VMEM((2560, 128), f32),
            pltpu.VMEM((2560, 128), f32),
            pltpu.VMEM((SUB, 640, 256), bf16),
            pltpu.VMEM((SUB, 4, 640, 256), bf16),
        ],
        compiler_params=pltpu.CompilerParams(
            dimension_semantics=("arbitrary",), vmem_limit_bytes=44 << 20
        ),
        name="slab",
    )(
        *map(in_hbm, [*conv, *[cotangent] * (2 * SUB)]), mixed, t["inverse_y"], t["inverse_z"],
        t["unscale_inverse"], t["forward_z"], t["forward_y"], t["unscale_back"],
    )


def small_call(kernel, name, out_shape, scratch, *args):
    return pl.pallas_call(
        kernel,
        out_shape=out_shape,
        scratch_shapes=scratch,
        compiler_params=pltpu.CompilerParams(vmem_limit_bytes=10 << 20),
        name=name,
    )(*args)


def lower_half():
    return lax.broadcasted_iota(jnp.int32, (64, 128), 1) < 64


def forward_x_kernel(in_ref, fx_ref, out_ref, wide_ref):
    low = lower_half()
    for gk in range(GA):
        cols = []
        for b in range(2):
            row = (2 * gk + b) * 16
            cols.append(jnp.concatenate([in_ref[j * 320 + row : j * 320 + row + 16, :] for j in range(8)], axis=0))
        right = jnp.concatenate(cols, axis=1)
        out = mm(fx_ref[...], jnp.concatenate([right, right], axis=0))
        first = jnp.where(low, out[:64, :128], out[64:, 128:])
        second = jnp.where(low, out[:64, 128:], out[64:, :128])
        res = first + pltpu.roll(second, 64, 1)
        for r in range(4):
            wide_ref[pl.ds(r * GA + gk, 16, stride=40), :] = res[r * 16 : (r + 1) * 16]
    out_ref[...] = wide_ref[...].astype(bf16)


def inverse_x_kernel(in_ref, ix_ref, out_ref, wide_ref):
    wide_ref[...] = in_ref[...].astype(f32)
    low = lax.broadcasted_iota(jnp.int32, (128, 128), 1) < 64
    for gk in range(GA):
        rows = [wide_ref[pl.ds(r * GA + gk, 16, stride=40), :] for r in range(4)]
        part = jnp.concatenate(rows, axis=0).astype(bf16)
        out = mm(ix_ref[...], jnp.concatenate([part, part], axis=0))
        first = jnp.where(low, out[:128], pltpu.roll(out[128:], 64, 1)).astype(bf16)
        second = jnp.where(low, pltpu.roll(out[:128], 64, 1), out[128:]).astype(bf16)
        for b, value in enumerate((first, second)):
            row = (2 * gk + b) * 16
            for j in range(8):
                out_ref[j * 320 + row : j * 320 + row + 16, :] = value[j * 16 : (j + 1) * 16]


def weight_kernel(w_ref, place_ref, out_ref, wide_ref):
    wide_ref[...] = w_ref[...].astype(f32)
    cols = [wide_ref[pl.ds(o, 400, stride=4), :].astype(bf16) for o in range(4)]
    out = mm(jnp.concatenate(cols, axis=1), place_ref[...])
    out_ref[0] = out[:, :128]
    out_ref[1] = out[:, 128:]


def spread_channels(in_ref, spread_ref, wide_ref, rows_ref, chan_ref):
    wide_ref[...] = in_ref[...].astype(f32)
    for r in range(40):
        rows_ref[r * 16 : (r + 1) * 16, :] = wide_ref[pl.ds(r, 16, stride=40), :].astype(bf16)
    chan_ref[...] = mm(rows_ref[...], spread_ref[...])


def channel_parts(chan_ref, kxl, kya, c):
    row = (kxl * 20 + (c // 4) * 2 + kya) * 16
    lanes = (c % 4) * 128
    return (
        chan_ref[row : row + 16, lanes : lanes + 128],
        chan_ref[row + 160 : row + 176, lanes : lanes + 128],
    )


SPREAD_SCRATCH = (
    pltpu.VMEM((640, 128), f32), pltpu.VMEM((640, 128), bf16), pltpu.VMEM((640, 512), f32)
)


def mix_kernel(in_ref, spread_ref, w_ref, out_ref, wide_ref, rows_ref, chan_ref):
    spread_channels(in_ref, spread_ref, wide_ref, rows_ref, chan_ref)
    for kxl in range(2):
        for kya in range(2):
            real = [jnp.zeros((16, 128), f32) for _ in range(G)]
            imag = [jnp.zeros((16, 128), f32) for _ in range(G)]
            for c in range(C):
                s_re, s_im = channel_parts(chan_ref, kxl, kya, c)
                for go in range(G):
                    line = kxl * 200 + c * G + go
                    w_re = w_ref[kya, line : line + 1, :]
                    w_im = w_ref[kya, line + 100 : line + 101, :]
                    real[go] = real[go] + (s_re * w_re - s_im * w_im)
                    imag[go] = imag[go] + (s_re * w_im + s_im * w_re)
            for go in range(G):
                row = kxl * 20 + go * 2 + kya
                wide_ref[pl.ds(row, 16, stride=40), :] = real[go]
                wide_ref[pl.ds(row + 10, 16, stride=40), :] = imag[go]
    out_ref[...] = wide_ref[...].astype(bf16)


def grad_kernel(s_ref, b_ref, spread_ref, gather_ref, out_ref, wide_ref, rows_ref, chan_ref, sum_ref):
    spread_channels(s_ref, spread_ref, wide_ref, rows_ref, chan_ref)
    wide_ref[...] = b_ref[...].astype(f32)
    for kxl in range(2):
        for kya in range(2):
            b_re = [wide_ref[pl.ds(kxl * 20 + g * 2 + kya, 16, stride=40), :] for g in range(G)]
            b_im = [wide_ref[pl.ds(kxl * 20 + g * 2 + kya + 10, 16, stride=40), :] for g in range(G)]
            for c in range(C):
                s_re, s_im = channel_parts(chan_ref, kxl, kya, c)
                for go in range(G):
                    line = kxl * 100 + c * G + go
                    real = s_re * b_re[go] + s_im * b_im[go]
                    imag = s_re * b_im[go] - s_im * b_re[go]
                    lanes = slice(kya * 128, kya * 128 + 128)
                    sum_ref[line : line + 1, lanes] = jnp.sum(real, axis=0, keepdims=True)
                    sum_ref[200 + line : 201 + line, lanes] = jnp.sum(imag, axis=0, keepdims=True)
    sums = sum_ref[...]
    upper = sums.astype(bf16)
    lower = (sums - upper.astype(f32)).astype(bf16)
    placed = mm(jnp.concatenate([upper, lower], axis=1), gather_ref[...])
    for o in range(4):
        for part in range(2):
            out_ref[pl.ds(o * 2 + part, 200, stride=8), :] = placed[
                part * 200 : (part + 1) * 200, o * 128 : o * 128 + 128
            ]


def exchange(values, axis, count):
    blocks = values.reshape(count, -1, 128)
    return lax.all_to_all(blocks, axis, split_axis=0, concat_axis=0, tiled=True).reshape(-1, 128)


def shards(fields, cotangent, spectral_weight, conv_weight, conv_bias):
    t = {name: jnp.asarray(value) for name, value in tables().items()}
    conv = (
        conv_weight.T[:, None, :, None] * jnp.eye(16, dtype=bf16)[None, :, None, :]
    ).reshape(320, 320)

    bias = jnp.broadcast_to(conv_bias[:, None, None], (C, 16, 128)).reshape(320, 128)

    def to_kx(modes):
        moved = exchange(modes, "mp", MP)
        part = small_call(
            forward_x_kernel, "forward_x", jax.ShapeDtypeStruct((640, 128), bf16),
            [pltpu.VMEM((640, 128), f32)], moved, t["forward_x"],
        )
        return exchange(part, "dp", DP)

    weights = small_call(
        weight_kernel, "weights", jax.ShapeDtypeStruct((2, 400, 128), f32),
        [pltpu.VMEM((1600, 64), f32)], spectral_weight.reshape(1600, 64), t["place"],
    )
    spectra = to_kx(analyse_call(fields, t))
    mixed = small_call(
        mix_kernel, "mix", jax.ShapeDtypeStruct((640, 128), bf16), SPREAD_SCRATCH,
        spectra, t["spread"], weights,
    )
    slabs = small_call(
        inverse_x_kernel, "inverse_x", jax.ShapeDtypeStruct((2560, 128), bf16),
        [pltpu.VMEM((640, 128), f32)], exchange(mixed, "dp", DP), t["inverse_x"],
    )
    slabs, conv = lax.optimization_barrier((slabs, conv))
    conv_term = conv_call(fields, conv, bias)
    back = to_kx(slab_call(conv_term, cotangent, exchange(slabs, "mp", MP), t))
    grad = small_call(
        grad_kernel, "grad", jax.ShapeDtypeStruct((1600, 128), f32),
        (*SPREAD_SCRATCH, pltpu.VMEM((400, 256), f32)), spectra, back, t["spread"], t["gather"],
    )
    return jnp.transpose(grad.reshape(2, C, C, 2, 128)[..., :64], (0, 3, 1, 2, 4))


def solution(mesh):
    return jax.shard_map(
        shards,
        mesh=mesh,
        in_specs=(
            P("dp", "mp", None, None, None),
            P("dp", "mp", None, None, None),
            P("dp", None, None, None, "mp"),
            P(),
            P(),
        ),
        out_specs=P("dp", None, None, None, "mp"),
        check_vma=False,
    )
```

```python
import functools

import jax
import jax.numpy as jnp
import ml_dtypes
import numpy as np
from jax import lax
from jax.experimental import pallas as pl
from jax.experimental.pallas import tpu as pltpu
from jax.sharding import PartitionSpec as P

X = 128
Y = 128
Z = 128
C = 20
KX = 32
KY = 32
KZ = 16
DP = 16
MP = 8
XP = 8
G = 5
GK = 20
GA = 10
SUB = 2

bf16 = jnp.bfloat16
f32 = jnp.float32
np_bf16 = ml_dtypes.bfloat16

INV_ROOT_TWO = 0.7071067811865476
TWO_OVER_ROOT_PI = 1.1283791670955126
LOG2_E = 1.4426950408889634


def kept(count, length):
    return np.concatenate([np.arange(count // 2), np.arange(length - count // 2, length)])


def angles(modes, length):
    return 2.0 * np.pi / length * ((modes[:, None] * np.arange(length)[None, :]) % length)


def hi_lo(table):
    upper = table.astype(np_bf16)
    lower = (table - upper.astype(np.float64)).astype(np_bf16)
    return upper, lower


def z_scales():
    candidates = 1.0 + np.arange(512) / 512
    scales = []
    for row in angles(np.arange(KZ), Z):
        values = np.concatenate([np.cos(row), np.sin(row)])[None, :] * candidates[:, None]
        off = ((values.astype(np_bf16).astype(np.float64) - values) ** 2).sum(1) / (values**2).sum(1)
        scales.append(candidates[int(np.argmin(off))])
    return np.array(scales)


@functools.cache
def tables():
    scale = z_scales()
    weight = np.where(np.arange(KZ) == 0, 1.0, 2.0) / (X * Y * Z)
    phase_z = angles(np.arange(KZ), Z)
    cos_z, sin_z = np.cos(phase_z), np.sin(phase_z)
    forward_z = np.zeros((8, Z, 2, 8, KZ))
    inverse_z = np.zeros((4, 2, 8, KZ, 2, Z))
    for q in range(8):
        forward_z[q, :, 0, q, :] = (cos_z * scale[:, None]).T
        forward_z[q, :, 1, q, :] = (sin_z * scale[:, None]).T
        inverse_z[q // 2, 0, q, :, q % 2, :] = cos_z * scale[:, None]
        inverse_z[q // 2, 1, q, :, q % 2, :] = -sin_z * scale[:, None]
    unscale = np.tile(1.0 / scale, 8)[None, :]
    unscale_back = np.tile(0.5 * weight / scale, 8)[None, :]
    unscale_inverse = np.tile(INV_ROOT_TWO * weight / scale, 8)[None, :]
    phase_y = angles(kept(KY, Y), Y)
    cos_y, sin_y = np.cos(phase_y), np.sin(phase_y)
    forward_y = np.zeros((KY, 2, 2, Y))
    forward_y[:, 0, 0], forward_y[:, 0, 1] = cos_y, -sin_y
    forward_y[:, 1, 0], forward_y[:, 1, 1] = -sin_y, -cos_y
    forward_y = np.concatenate(hi_lo(forward_y.reshape(64, 256)), axis=0)
    inverse_y = np.zeros((2, Y, KY, 2))
    inverse_y[0, :, :, 0], inverse_y[0, :, :, 1] = cos_y.T, -sin_y.T
    inverse_y[1, :, :, 0], inverse_y[1, :, :, 1] = sin_y.T, cos_y.T
    inverse_y = np.concatenate(hi_lo(inverse_y.reshape(256, 64)), axis=1)
    phase_x = angles(kept(KX, X), X).reshape(16, 2, 8, 8, 2)
    cos_x, sin_x = np.cos(phase_x), np.sin(phase_x)
    forward_x = np.zeros((2, 2, 2, 16, 8, 2, 8))
    inverse_x = np.zeros((2, 8, 2, 8, 2, 2, 16))
    cos_f = np.transpose(cos_x, (4, 1, 0, 2, 3))
    sin_f = np.transpose(sin_x, (4, 1, 0, 2, 3))
    forward_x[:, :, 0, :, :, 0, :] = cos_f
    forward_x[:, :, 0, :, :, 1, :] = sin_f
    forward_x[:, :, 1, :, :, 0, :] = -sin_f
    forward_x[:, :, 1, :, :, 1, :] = cos_f
    cos_i = np.transpose(cos_x, (4, 2, 3, 1, 0))
    sin_i = np.transpose(sin_x, (4, 2, 3, 1, 0))
    inverse_x[:, :, 0, :, :, 0, :] = cos_i
    inverse_x[:, :, 0, :, :, 1, :] = -sin_i
    inverse_x[:, :, 1, :, :, 0, :] = sin_i
    inverse_x[:, :, 1, :, :, 1, :] = cos_i
    forward_x = np.concatenate(hi_lo(forward_x.reshape(128, 128)), axis=1)
    inverse_x = np.concatenate(hi_lo(inverse_x.reshape(256, 64)), axis=1)
    spread = np.zeros((2, 4, KZ, 4, 2, 4, KZ))
    for channel in range(4):
        for place in range(4):
            for b in range(2):
                spread[b, channel, np.arange(KZ), channel, b, place, np.arange(KZ)] = 1.0
    spread = spread.reshape(128, 512)
    place = np.zeros((4, 4, KZ, 2, 2, 4, KZ))
    for o in range(4):
        for kyl in range(4):
            place[o, kyl, np.arange(KZ), kyl // 2, kyl % 2, o, np.arange(KZ)] = 1.0
    gather = np.zeros((2, 2, 4, KZ, 4, 2, 2, 2, KZ))
    for o in range(4):
        for a in range(2):
            for b in range(2):
                gather[a, b, o, np.arange(KZ), o, 0, a, b, np.arange(KZ)] = 1.0
    gather = gather.reshape(256, 512)
    return dict(
        gather=np.concatenate([gather, gather], axis=0).astype(np_bf16),
        forward_z=forward_z.reshape(4, 256, 256).astype(np_bf16),
        inverse_z=inverse_z.reshape(4, 256, 256).astype(np_bf16),
        unscale=unscale.astype(np.float32),
        unscale_back=unscale_back.astype(np.float32),
        unscale_inverse=unscale_inverse.astype(np.float32),
        forward_y=forward_y,
        inverse_y=inverse_y,
        forward_x=forward_x,
        inverse_x=inverse_x,
        spread=spread.astype(np_bf16),
        place=place.reshape(256, 256).astype(np_bf16),
    )


def mm(a, b):
    return jnp.dot(a, b, preferred_element_type=f32)


def z_transform(lhs_of, fz_ref, groups):
    total = mm(lhs_of(0, groups), fz_ref[0])
    for pair in range(1, 4):
        total = total + mm(lhs_of(pair, groups), fz_ref[pair])
    return total


def y_transform(part, fy_ref, modes_ref, g, at):
    both = jnp.concatenate([part[:, :128], part[:, 128:]], axis=0)
    upper = both.astype(bf16)
    lower = (both - upper.astype(f32)).astype(bf16)
    out = mm(fy_ref[...], jnp.concatenate([upper, lower], axis=1))
    modes = out[:64, :128] + out[64:, :128] + out[:64, 128:]
    for j in range(MP):
        modes_ref[pl.ds(j * 320 + g * 64 + at, 8, stride=8), :] = modes[j * 8 : (j + 1) * 8]


def analyse(lhs_of, fz_ref, fy_ref, modes_ref, at, groups):
    total = z_transform(lhs_of, fz_ref, groups)
    for k, g in enumerate(groups):
        y_transform(total[k * Y : (k + 1) * Y], fy_ref, modes_ref, g, at)


HALVES = ((0, 1, 2), (3, 4))


def analyse_kernel(*refs):
    field_refs, (fz_ref, fy_ref, out_ref, modes_ref) = refs[: 2 * SUB], refs[2 * SUB :]
    step = pl.program_id(0)

    def lhs_of(sub):
        def lhs(pair, groups):
            xl, c4 = 2 * sub + pair // 2, 2 * (pair % 2)
            rows = [
                jnp.concatenate(
                    [field_refs[xl][0, 0, 4 * g + c4], field_refs[xl][0, 0, 4 * g + c4 + 1]], axis=1
                )
                for g in groups
            ]
            return jnp.concatenate(rows, axis=0)

        return lhs

    totals = [z_transform(lhs_of(sub), fz_ref, range(G)) for sub in range(SUB)]
    for g in range(G):
        for sub in range(SUB):
            y_transform(totals[sub][g * Y : (g + 1) * Y], fy_ref, modes_ref, g, step * SUB + sub)

    @pl.when(step == XP // SUB - 1)
    def _():
        out_ref[...] = modes_ref[...].astype(bf16)


def x_streams():
    return [
        pl.BlockSpec((1, 1, C, Y, Z), lambda i, k=k: (0, 2 * SUB * i + k, 0, 0, 0))
        for k in range(2 * SUB)
    ]


def in_hbm(array):
    return pltpu.with_memory_space_constraint(array, pltpu.HBM)


def full(shape):
    zeros = (0,) * len(shape)
    return pl.BlockSpec(shape, lambda *_: zeros, pipeline_mode=pl.Buffered(1))


def analyse_call(fields, t):
    return pl.pallas_call(
        analyse_kernel,
        out_shape=jax.ShapeDtypeStruct((2560, 128), bf16),
        grid=(XP // SUB,),
        in_specs=[
            *x_streams(),
            full((4, 256, 256)),
            full((128, 256)),
        ],
        out_specs=pl.BlockSpec((2560, 128), lambda i: (0, 0)),
        scratch_shapes=[pltpu.VMEM((2560, 128), f32)],
        compiler_params=pltpu.CompilerParams(
            dimension_semantics=("arbitrary",), vmem_limit_bytes=44 << 20
        ),
        name="analyse",
    )(*map(in_hbm, [*[fields] * (2 * SUB), t["forward_z"], t["forward_y"]]))


def conv_kernel(*refs):
    field_refs, (conv_ref, bias_ref), out_refs = refs[: 2 * SUB], refs[2 * SUB : -2 * SUB], refs[-2 * SUB :]
    bias = jnp.concatenate([bias_ref[...], bias_ref[...]], axis=1)
    for xl in range(2 * SUB):
        for yp in range(4):
            right = jnp.concatenate(
                [
                    field_refs[xl][0, 0, :, yp * 32 + h * 16 : yp * 32 + (h + 1) * 16, :].reshape(320, Z)
                    for h in range(2)
                ],
                axis=1,
            )
            out = ((mm(conv_ref[...], right) + bias) * INV_ROOT_TWO).astype(bf16)
            for h in range(2):
                out_refs[xl][0, :, yp * 32 + h * 16 : yp * 32 + (h + 1) * 16, :] = out[
                    :, h * 128 : (h + 1) * 128
                ].reshape(C, 16, Z)


def conv_call(fields, conv, bias):
    return pl.pallas_call(
        conv_kernel,
        out_shape=[pltpu.HBM((XP // SUB, C, Y, Z), bf16)] * (2 * SUB),
        grid=(XP // SUB,),
        in_specs=[
            *x_streams(),
            full((320, 320)),
            full((320, 128)),
        ],
        out_specs=[pl.BlockSpec((1, C, Y, Z), lambda i: (i, 0, 0, 0))] * (2 * SUB),
        compiler_params=pltpu.CompilerParams(
            dimension_semantics=("arbitrary",), vmem_limit_bytes=44 << 20
        ),
        cost_estimate=pl.CostEstimate(
            flops=2 * 16 * Y * Z * 320 * C, bytes_accessed=4 * 16 * C * Y * Z, transcendentals=0
        ),
        name="conv",
    )(*map(in_hbm, [fields] * (2 * SUB)), conv, bias)


def slab_kernel(*refs):
    conv_refs, cot_refs = refs[: 2 * SUB], refs[2 * SUB : 4 * SUB]
    mixed_ref, iy_ref, iz_ref, fz_ref, fy_ref, out_ref = refs[4 * SUB : 4 * SUB + 6]
    modes_ref, mixed_f32, wave_ref, delta_ref = refs[4 * SUB + 6 :]
    step = pl.program_id(0)

    def wave(at, slot, g):
        rows = [mixed_f32[pl.ds(j * 320 + g * 64 + at, 8, stride=8), :] for j in range(MP)]
        part = jnp.concatenate(rows, axis=0).astype(bf16)
        out = mm(iy_ref[...], jnp.concatenate([part, part], axis=0))
        out = out.astype(bf16)
        wave_ref[slot, g * Y : (g + 1) * Y, :128] = out[:Y]
        wave_ref[slot, g * Y : (g + 1) * Y, 128:] = out[Y:]

    def delta(sub, pair, spectral):
        xl = 2 * sub + pair // 2
        for g in range(G):
            for h in range(2):
                channel = 4 * g + 2 * (pair % 2) + h
                u = spectral[g * Y : (g + 1) * Y, h * 128 : (h + 1) * 128] + conv_refs[xl][
                    0, channel
                ].astype(f32)
                bell = jnp.exp2(u * u * -LOG2_E)
                slope = 1.0 + (lax.erf(u) + (u * TWO_OVER_ROOT_PI) * bell)
                value = cot_refs[xl][0, 0, channel].astype(f32) * slope
                delta_ref[sub % 2, pair, g * Y : (g + 1) * Y, h * 128 : (h + 1) * 128] = value.astype(bf16)

    def lhs_of(slot):
        return lambda pair, groups: delta_ref[slot, pair, groups[0] * Y : (groups[-1] + 1) * Y, :]

    @pl.when(step == 0)
    def _():
        mixed_f32[...] = mixed_ref[...].astype(f32)
        for g in range(G):
            wave(0, 0, g)

    for sub in range(SUB):
        at = step * SUB + sub
        before = jnp.maximum(at - 1, 0)
        after = jnp.minimum(at + 1, XP - 1)
        slot = sub % 2
        lhs = lhs_of(1 - slot)
        spectral = [mm(wave_ref[slot], iz_ref[0])]
        totals = []
        for pair in range(4):
            if pair < 3:
                spectral.append(mm(wave_ref[slot], iz_ref[pair + 1]))
            delta(sub, pair, spectral[pair])
            if pair < 2:
                totals.append(z_transform(lhs, fz_ref, HALVES[pair]))
            else:
                for k, g in enumerate(HALVES[pair - 2]):
                    y_transform(totals[pair - 2][k * Y : (k + 1) * Y], fy_ref, modes_ref, g, before)
            for g in ((0, 1), (2,), (3,), (4,))[pair]:
                wave(after, 1 - slot, g)

    @pl.when(step == XP // SUB - 1)
    def _():
        lhs = lhs_of((SUB - 1) % 2)
        for groups in HALVES:
            analyse(lhs, fz_ref, fy_ref, modes_ref, XP - 1, groups)
        out_ref[...] = modes_ref[...].astype(bf16)


def slab_call(conv, cotangent, mixed, t):
    return pl.pallas_call(
        slab_kernel,
        out_shape=jax.ShapeDtypeStruct((2560, 128), bf16),
        grid=(XP // SUB,),
        in_specs=[
            *[pl.BlockSpec((1, C, Y, Z), lambda i: (i, 0, 0, 0))] * (2 * SUB),
            *x_streams(),
            full((2560, 128)),
            full((256, 128)),
            full((4, 256, 256)),
            full((4, 256, 256)),
            full((128, 256)),
        ],
        out_specs=pl.BlockSpec((2560, 128), lambda i: (0, 0)),
        scratch_shapes=[
            pltpu.VMEM((2560, 128), f32),
            pltpu.VMEM((2560, 128), f32),
            pltpu.VMEM((SUB, 640, 256), bf16),
            pltpu.VMEM((SUB, 4, 640, 256), bf16),
        ],
        compiler_params=pltpu.CompilerParams(
            dimension_semantics=("arbitrary",), vmem_limit_bytes=44 << 20
        ),
        name="slab",
    )(
        *map(in_hbm, [*conv, *[cotangent] * (2 * SUB)]), mixed, t["inverse_y"], t["inverse_z"],
        t["forward_z"], t["forward_y"],
    )


def small_call(kernel, name, out_shape, scratch, *args):
    return pl.pallas_call(
        kernel,
        out_shape=out_shape,
        scratch_shapes=scratch,
        compiler_params=pltpu.CompilerParams(vmem_limit_bytes=10 << 20),
        name=name,
    )(*args)


def lower_half():
    return lax.broadcasted_iota(jnp.int32, (64, 128), 1) < 64


def forward_x_kernel(in_ref, fx_ref, un_ref, out_ref, wide_ref):
    low = lower_half()
    for gk in range(GA):
        cols = []
        for b in range(2):
            row = (2 * gk + b) * 16
            cols.append(jnp.concatenate([in_ref[j * 320 + row : j * 320 + row + 16, :] for j in range(8)], axis=0))
        right = jnp.concatenate(cols, axis=1)
        out = mm(fx_ref[...], jnp.concatenate([right, right], axis=0))
        first = jnp.where(low, out[:64, :128], out[64:, 128:])
        second = jnp.where(low, out[:64, 128:], out[64:, :128])
        res = (first + pltpu.roll(second, 64, 1)) * un_ref[...]
        for r in range(4):
            wide_ref[pl.ds(r * GA + gk, 16, stride=40), :] = res[r * 16 : (r + 1) * 16]
    out_ref[...] = wide_ref[...].astype(bf16)


def inverse_x_kernel(in_ref, ix_ref, un_ref, out_ref, wide_ref):
    wide_ref[...] = in_ref[...].astype(f32)
    low = lax.broadcasted_iota(jnp.int32, (128, 128), 1) < 64
    for gk in range(GA):
        rows = [wide_ref[pl.ds(r * GA + gk, 16, stride=40), :] for r in range(4)]
        part = jnp.concatenate(rows, axis=0).astype(bf16)
        out = mm(ix_ref[...], jnp.concatenate([part, part], axis=0)) * un_ref[...]
        first = jnp.where(low, out[:128], pltpu.roll(out[128:], 64, 1)).astype(bf16)
        second = jnp.where(low, pltpu.roll(out[:128], 64, 1), out[128:]).astype(bf16)
        for b, value in enumerate((first, second)):
            row = (2 * gk + b) * 16
            for j in range(8):
                out_ref[j * 320 + row : j * 320 + row + 16, :] = value[j * 16 : (j + 1) * 16]


def weight_kernel(w_ref, place_ref, out_ref, wide_ref):
    wide_ref[...] = w_ref[...].astype(f32)
    cols = [wide_ref[pl.ds(o, 400, stride=4), :].astype(bf16) for o in range(4)]
    out = mm(jnp.concatenate(cols, axis=1), place_ref[...])
    out_ref[0] = out[:, :128]
    out_ref[1] = out[:, 128:]


def spread_channels(in_ref, spread_ref, wide_ref, rows_ref, chan_ref):
    wide_ref[...] = in_ref[...].astype(f32)
    for r in range(40):
        rows_ref[r * 16 : (r + 1) * 16, :] = wide_ref[pl.ds(r, 16, stride=40), :].astype(bf16)
    chan_ref[...] = mm(rows_ref[...], spread_ref[...])


def channel_parts(chan_ref, kxl, kya, c):
    row = (kxl * 20 + (c // 4) * 2 + kya) * 16
    lanes = (c % 4) * 128
    return (
        chan_ref[row : row + 16, lanes : lanes + 128],
        chan_ref[row + 160 : row + 176, lanes : lanes + 128],
    )


SPREAD_SCRATCH = (
    pltpu.VMEM((640, 128), f32), pltpu.VMEM((640, 128), bf16), pltpu.VMEM((640, 512), f32)
)


def mix_kernel(in_ref, spread_ref, w_ref, out_ref, wide_ref, rows_ref, chan_ref):
    spread_channels(in_ref, spread_ref, wide_ref, rows_ref, chan_ref)
    for kxl in range(2):
        for kya in range(2):
            real = [jnp.zeros((16, 128), f32) for _ in range(G)]
            imag = [jnp.zeros((16, 128), f32) for _ in range(G)]
            for c in range(C):
                s_re, s_im = channel_parts(chan_ref, kxl, kya, c)
                for go in range(G):
                    line = kxl * 200 + c * G + go
                    w_re = w_ref[kya, line : line + 1, :]
                    w_im = w_ref[kya, line + 100 : line + 101, :]
                    real[go] = real[go] + (s_re * w_re - s_im * w_im)
                    imag[go] = imag[go] + (s_re * w_im + s_im * w_re)
            for go in range(G):
                row = kxl * 20 + go * 2 + kya
                wide_ref[pl.ds(row, 16, stride=40), :] = real[go]
                wide_ref[pl.ds(row + 10, 16, stride=40), :] = imag[go]
    out_ref[...] = wide_ref[...].astype(bf16)


def grad_kernel(
    s_ref, b_ref, spread_ref, gather_ref, out_ref, wide_ref, rows_ref, chan_ref, line_ref, sum_ref
):
    spread_channels(s_ref, spread_ref, wide_ref, rows_ref, chan_ref)
    for r in range(40):
        for c4 in range(4):
            kxl, part, g, kya = r // 20, r // 10 % 2, r // 2 % 5, r % 2
            first = ((kxl * 2 + part) * 2 + kya) * 384 + 4 * g + c4
            line_ref[pl.ds(first, 16, stride=24), :] = chan_ref[
                r * 16 : (r + 1) * 16, c4 * 128 : (c4 + 1) * 128
            ]
    wide_ref[...] = b_ref[...].astype(f32)
    for kxl in range(2):
        for kya in range(2):
            base = (kxl * 4 + kya) * 384
            for go in range(G):
                real = jnp.zeros((24, 128), f32)
                imag = jnp.zeros((24, 128), f32)
                for s in range(DP):
                    row = s * 40 + kxl * 20 + go * 2 + kya
                    b_re = wide_ref[row : row + 1, :]
                    b_im = wide_ref[row + 10 : row + 11, :]
                    s_re = line_ref[base + s * 24 : base + s * 24 + 24, :]
                    s_im = line_ref[base + 768 + s * 24 : base + 768 + s * 24 + 24, :]
                    real = real + (s_re * b_re + s_im * b_im)
                    imag = imag + (s_re * b_im - s_im * b_re)
                first = kya * 400 + kxl * 100 + go
                sum_ref[pl.ds(first, C, stride=G), :] = real[:C]
                sum_ref[pl.ds(first + 200, C, stride=G), :] = imag[:C]
    sums = jnp.concatenate([sum_ref[:400, :], sum_ref[400:, :]], axis=1)
    upper = sums.astype(bf16)
    lower = (sums - upper.astype(f32)).astype(bf16)
    placed = mm(jnp.concatenate([upper, lower], axis=1), gather_ref[...])
    for o in range(4):
        for part in range(2):
            line_ref[pl.ds(o * 2 + part, 200, stride=8), :] = placed[
                part * 200 : (part + 1) * 200, o * 128 : o * 128 + 128
            ]
    out_ref[...] = line_ref[:1600, :64]


def exchange(values, axis, count):
    blocks = values.reshape(count, -1, 128)
    return lax.all_to_all(blocks, axis, split_axis=0, concat_axis=0, tiled=True).reshape(-1, 128)


def shards(fields, cotangent, spectral_weight, conv_weight, conv_bias):
    t = {name: jnp.asarray(value) for name, value in tables().items()}
    conv = (
        conv_weight.T[:, None, :, None] * jnp.eye(16, dtype=bf16)[None, :, None, :]
    ).reshape(320, 320)

    bias = jnp.broadcast_to(conv_bias[:, None, None], (C, 16, 128)).reshape(320, 128)

    def to_kx(modes, unscale):
        moved = exchange(modes, "mp", MP)
        part = small_call(
            forward_x_kernel, "forward_x", jax.ShapeDtypeStruct((640, 128), bf16),
            [pltpu.VMEM((640, 128), f32)], moved, t["forward_x"], unscale,
        )
        return exchange(part, "dp", DP)

    weights = small_call(
        weight_kernel, "weights", jax.ShapeDtypeStruct((2, 400, 128), f32),
        [pltpu.VMEM((1600, 64), f32)], spectral_weight.reshape(1600, 64), t["place"],
    )
    weights, conv, bias = lax.optimization_barrier((weights, conv, bias))
    spectra = to_kx(analyse_call(fields, t), t["unscale"])
    mixed = small_call(
        mix_kernel, "mix", jax.ShapeDtypeStruct((640, 128), bf16), SPREAD_SCRATCH,
        spectra, t["spread"], weights,
    )
    slabs = small_call(
        inverse_x_kernel, "inverse_x", jax.ShapeDtypeStruct((2560, 128), bf16),
        [pltpu.VMEM((640, 128), f32)], exchange(mixed, "dp", DP), t["inverse_x"], t["unscale_inverse"],
    )
    slabs, conv = lax.optimization_barrier((slabs, conv))
    conv_term = conv_call(fields, conv, bias)
    back = to_kx(slab_call(conv_term, cotangent, exchange(slabs, "mp", MP), t), t["unscale_back"])
    grad = small_call(
        grad_kernel, "grad", jax.ShapeDtypeStruct((1600, 64), f32),
        (*SPREAD_SCRATCH, pltpu.VMEM((3072, 128), f32), pltpu.VMEM((800, 128), f32)), spectra, back, t["spread"], t["gather"],
    )
    return jnp.transpose(grad.reshape(2, C, C, 2, 64), (0, 3, 1, 2, 4))


def solution(mesh):
    return jax.shard_map(
        shards,
        mesh=mesh,
        in_specs=(
            P("dp", "mp", None, None, None),
            P("dp", "mp", None, None, None),
            P("dp", None, None, None, "mp"),
            P(),
            P(),
        ),
        out_specs=P("dp", None, None, None, "mp"),
        check_vma=False,
    )
```

```python
import functools

import jax
import jax.numpy as jnp
import ml_dtypes
import numpy as np
from jax import lax
from jax.experimental import pallas as pl
from jax.experimental.pallas import tpu as pltpu
from jax.sharding import PartitionSpec as P

X = 128
Y = 128
Z = 128
C = 20
KX = 32
KY = 32
KZ = 16
DP = 16
MP = 8
XP = 8
G = 5
GK = 20
GA = 10
SUB = 2

bf16 = jnp.bfloat16
f32 = jnp.float32
np_bf16 = ml_dtypes.bfloat16

INV_ROOT_TWO = 0.7071067811865476
TWO_OVER_ROOT_PI = 1.1283791670955126
LOG2_E = 1.4426950408889634


def kept(count, length):
    return np.concatenate([np.arange(count // 2), np.arange(length - count // 2, length)])


def angles(modes, length):
    return 2.0 * np.pi / length * ((modes[:, None] * np.arange(length)[None, :]) % length)


def hi_lo(table):
    upper = table.astype(np_bf16)
    lower = (table - upper.astype(np.float64)).astype(np_bf16)
    return upper, lower


def z_scales():
    candidates = 1.0 + np.arange(512) / 512
    scales = []
    for row in angles(np.arange(KZ), Z):
        values = np.concatenate([np.cos(row), np.sin(row)])[None, :] * candidates[:, None]
        off = ((values.astype(np_bf16).astype(np.float64) - values) ** 2).sum(1) / (values**2).sum(1)
        scales.append(candidates[int(np.argmin(off))])
    return np.array(scales)


@functools.cache
def tables():
    scale = z_scales()
    weight = np.where(np.arange(KZ) == 0, 1.0, 2.0) / (X * Y * Z)
    phase_z = angles(np.arange(KZ), Z)
    cos_z, sin_z = np.cos(phase_z), np.sin(phase_z)
    forward_z = np.zeros((8, Z, 2, 8, KZ))
    inverse_z = np.zeros((4, 2, 8, KZ, 2, Z))
    for q in range(8):
        forward_z[q, :, 0, q, :] = (cos_z * scale[:, None]).T
        forward_z[q, :, 1, q, :] = (sin_z * scale[:, None]).T
        inverse_z[q // 2, 0, q, :, q % 2, :] = cos_z * scale[:, None]
        inverse_z[q // 2, 1, q, :, q % 2, :] = -sin_z * scale[:, None]
    unscale = np.tile(1.0 / scale, 8)[None, :]
    unscale_back = np.tile(0.5 * weight / scale, 8)[None, :]
    unscale_inverse = np.tile(INV_ROOT_TWO * weight / scale, 8)[None, :]
    phase_y = angles(kept(KY, Y), Y)
    cos_y, sin_y = np.cos(phase_y), np.sin(phase_y)
    forward_y = np.zeros((KY, 2, 2, Y))
    forward_y[:, 0, 0], forward_y[:, 0, 1] = cos_y, -sin_y
    forward_y[:, 1, 0], forward_y[:, 1, 1] = -sin_y, -cos_y
    forward_y = np.concatenate(hi_lo(forward_y.reshape(64, 256)), axis=0)
    inverse_y = np.zeros((2, Y, KY, 2))
    inverse_y[0, :, :, 0], inverse_y[0, :, :, 1] = cos_y.T, -sin_y.T
    inverse_y[1, :, :, 0], inverse_y[1, :, :, 1] = sin_y.T, cos_y.T
    inverse_y = np.concatenate(hi_lo(inverse_y.reshape(256, 64)), axis=1)
    phase_x = angles(kept(KX, X), X).reshape(16, 2, 8, 8, 2)
    cos_x, sin_x = np.cos(phase_x), np.sin(phase_x)
    forward_x = np.zeros((2, 2, 2, 16, 8, 2, 8))
    inverse_x = np.zeros((2, 8, 2, 8, 2, 2, 16))
    cos_f = np.transpose(cos_x, (4, 1, 0, 2, 3))
    sin_f = np.transpose(sin_x, (4, 1, 0, 2, 3))
    forward_x[:, :, 0, :, :, 0, :] = cos_f
    forward_x[:, :, 0, :, :, 1, :] = sin_f
    forward_x[:, :, 1, :, :, 0, :] = -sin_f
    forward_x[:, :, 1, :, :, 1, :] = cos_f
    cos_i = np.transpose(cos_x, (4, 2, 3, 1, 0))
    sin_i = np.transpose(sin_x, (4, 2, 3, 1, 0))
    inverse_x[:, :, 0, :, :, 0, :] = cos_i
    inverse_x[:, :, 0, :, :, 1, :] = -sin_i
    inverse_x[:, :, 1, :, :, 0, :] = sin_i
    inverse_x[:, :, 1, :, :, 1, :] = cos_i
    forward_x = np.concatenate(hi_lo(forward_x.reshape(128, 128)), axis=1)
    inverse_x = np.concatenate(hi_lo(inverse_x.reshape(256, 64)), axis=1)
    spread = np.zeros((2, 4, KZ, 4, 2, 4, KZ))
    for channel in range(4):
        for place in range(4):
            for b in range(2):
                spread[b, channel, np.arange(KZ), channel, b, place, np.arange(KZ)] = 1.0
    spread = spread.reshape(128, 512)
    place = np.zeros((4, 4, KZ, 2, 2, 4, KZ))
    for o in range(4):
        for kyl in range(4):
            place[o, kyl, np.arange(KZ), kyl // 2, kyl % 2, o, np.arange(KZ)] = 1.0
    gather = np.zeros((2, 2, 4, KZ, 4, 2, 2, 2, KZ))
    for o in range(4):
        for a in range(2):
            for b in range(2):
                gather[a, b, o, np.arange(KZ), o, 0, a, b, np.arange(KZ)] = 1.0
    gather = gather.reshape(256, 512)
    return dict(
        gather=np.concatenate([gather, gather], axis=0).astype(np_bf16),
        forward_z=forward_z.reshape(4, 256, 256).astype(np_bf16),
        inverse_z=inverse_z.reshape(4, 256, 256).astype(np_bf16),
        unscale=unscale.astype(np.float32),
        unscale_back=unscale_back.astype(np.float32),
        unscale_inverse=unscale_inverse.astype(np.float32),
        forward_y=forward_y,
        inverse_y=inverse_y,
        forward_x=forward_x,
        inverse_x=inverse_x,
        spread=spread.astype(np_bf16),
        place=place.reshape(256, 256).astype(np_bf16),
    )


def mm(a, b):
    return jnp.dot(a, b, preferred_element_type=f32)


def z_transform(lhs_of, fz_ref, groups):
    total = mm(lhs_of(0, groups), fz_ref[0])
    for pair in range(1, 4):
        total = total + mm(lhs_of(pair, groups), fz_ref[pair])
    return total


def y_transform(part, fy_ref, modes_ref, g, at):
    both = jnp.concatenate([part[:, :128], part[:, 128:]], axis=0)
    upper = both.astype(bf16)
    lower = (both - upper.astype(f32)).astype(bf16)
    out = mm(fy_ref[...], jnp.concatenate([upper, lower], axis=1))
    modes = out[:64, :128] + out[64:, :128] + out[:64, 128:]
    for j in range(MP):
        modes_ref[pl.ds(j * 320 + g * 64 + at, 8, stride=8), :] = modes[j * 8 : (j + 1) * 8]


def analyse(lhs_of, fz_ref, fy_ref, modes_ref, at, groups):
    total = z_transform(lhs_of, fz_ref, groups)
    for k, g in enumerate(groups):
        y_transform(total[k * Y : (k + 1) * Y], fy_ref, modes_ref, g, at)


HALVES = ((0, 1, 2), (3, 4))


def analyse_kernel(*refs):
    field_refs, (fz_ref, fy_ref, out_ref, modes_ref) = refs[: 2 * SUB], refs[2 * SUB :]
    step = pl.program_id(0)

    def lhs_of(sub):
        def lhs(pair, groups):
            xl, c4 = 2 * sub + pair // 2, 2 * (pair % 2)
            rows = [
                jnp.concatenate(
                    [field_refs[xl][0, 0, 4 * g + c4], field_refs[xl][0, 0, 4 * g + c4 + 1]], axis=1
                )
                for g in groups
            ]
            return jnp.concatenate(rows, axis=0)

        return lhs

    totals = [z_transform(lhs_of(sub), fz_ref, range(G)) for sub in range(SUB)]
    for g in range(G):
        for sub in range(SUB):
            y_transform(totals[sub][g * Y : (g + 1) * Y], fy_ref, modes_ref, g, step * SUB + sub)

    @pl.when(step == XP // SUB - 1)
    def _():
        out_ref[...] = modes_ref[...].astype(bf16)


def x_streams():
    return [
        pl.BlockSpec((1, 1, C, Y, Z), lambda i, k=k: (0, 2 * SUB * i + k, 0, 0, 0))
        for k in range(2 * SUB)
    ]


def in_hbm(array):
    return pltpu.with_memory_space_constraint(array, pltpu.HBM)


def full(shape):
    zeros = (0,) * len(shape)
    return pl.BlockSpec(shape, lambda *_: zeros, pipeline_mode=pl.Buffered(1))


def analyse_call(fields, t):
    return pl.pallas_call(
        analyse_kernel,
        out_shape=jax.ShapeDtypeStruct((2560, 128), bf16),
        grid=(XP // SUB,),
        in_specs=[
            *x_streams(),
            full((4, 256, 256)),
            full((128, 256)),
        ],
        out_specs=pl.BlockSpec((2560, 128), lambda i: (0, 0)),
        scratch_shapes=[pltpu.VMEM((2560, 128), f32)],
        compiler_params=pltpu.CompilerParams(
            dimension_semantics=("arbitrary",), vmem_limit_bytes=44 << 20
        ),
        name="analyse",
    )(*map(in_hbm, [*[fields] * (2 * SUB), t["forward_z"], t["forward_y"]]))


def conv_kernel(*refs):
    field_refs, (w_ref, bias_ref) = refs[: 2 * SUB], refs[2 * SUB : 2 * SUB + 2]
    out_refs, (conv_ref, lines_ref) = refs[2 * SUB + 2 : 4 * SUB + 2], refs[4 * SUB + 2 :]

    @pl.when(pl.program_id(0) == 0)
    def _():
        def picks(shape, along):
            long = lax.broadcasted_iota(jnp.int32, shape, along) >> 4
            return jnp.where(long == lax.broadcasted_iota(jnp.int32, shape, 1 - along), 1.0, 0.0).astype(bf16)

        by_row = lax.dot_general(
            picks((320, C), 0), w_ref[...], (((1,), (1,)), ((), ())), preferred_element_type=f32
        ).astype(bf16)
        spread = mm(by_row, picks((C, 320), 1))
        row = lax.broadcasted_iota(jnp.int32, (320, 320), 0) & 15
        column = lax.broadcasted_iota(jnp.int32, (320, 320), 1) & 15
        conv_ref[...] = jnp.where(row == column, spread, 0.0).astype(bf16)
        for o in range(C):
            lines_ref[o * 16 : (o + 1) * 16, :] = jnp.full((16, 256), bias_ref[o], f32)

    bias = lines_ref[...]
    for xl in range(2 * SUB):
        for yp in range(4):
            right = jnp.concatenate(
                [
                    field_refs[xl][0, 0, :, yp * 32 + h * 16 : yp * 32 + (h + 1) * 16, :].reshape(320, Z)
                    for h in range(2)
                ],
                axis=1,
            )
            out = ((mm(conv_ref[...], right) + bias) * INV_ROOT_TWO).astype(bf16)
            for h in range(2):
                out_refs[xl][0, :, yp * 32 + h * 16 : yp * 32 + (h + 1) * 16, :] = out[
                    :, h * 128 : (h + 1) * 128
                ].reshape(C, 16, Z)


def conv_call(fields, conv, bias):
    return pl.pallas_call(
        conv_kernel,
        out_shape=[pltpu.HBM((XP // SUB, C, Y, Z), bf16)] * (2 * SUB),
        grid=(XP // SUB,),
        in_specs=[
            *x_streams(),
            full((C, C)),
            pl.BlockSpec(memory_space=pltpu.SMEM),
        ],
        out_specs=[pl.BlockSpec((1, C, Y, Z), lambda i: (i, 0, 0, 0))] * (2 * SUB),
        scratch_shapes=[pltpu.VMEM((320, 320), bf16), pltpu.VMEM((320, 256), f32)],
        compiler_params=pltpu.CompilerParams(
            dimension_semantics=("arbitrary",), vmem_limit_bytes=44 << 20
        ),
        cost_estimate=pl.CostEstimate(
            flops=2 * 16 * Y * Z * 320 * C, bytes_accessed=4 * 16 * C * Y * Z, transcendentals=0
        ),
        name="conv",
    )(*map(in_hbm, [fields] * (2 * SUB)), conv, bias)


def slab_kernel(*refs):
    conv_refs, cot_refs = refs[: 2 * SUB], refs[2 * SUB : 4 * SUB]
    mixed_ref, iy_ref, iz_ref, fz_ref, fy_ref, out_ref = refs[4 * SUB : 4 * SUB + 6]
    modes_ref, mixed_f32, wave_ref, delta_ref = refs[4 * SUB + 6 :]
    step = pl.program_id(0)

    def wave(at, slot, g):
        rows = [mixed_f32[pl.ds(j * 320 + g * 64 + at, 8, stride=8), :] for j in range(MP)]
        part = jnp.concatenate(rows, axis=0).astype(bf16)
        out = mm(iy_ref[...], jnp.concatenate([part, part], axis=0))
        out = out.astype(bf16)
        wave_ref[slot, g * Y : (g + 1) * Y, :128] = out[:Y]
        wave_ref[slot, g * Y : (g + 1) * Y, 128:] = out[Y:]

    def delta(sub, pair, spectral):
        xl = 2 * sub + pair // 2
        for g in range(G):
            for h in range(2):
                channel = 4 * g + 2 * (pair % 2) + h
                u = spectral[g * Y : (g + 1) * Y, h * 128 : (h + 1) * 128] + conv_refs[xl][
                    0, channel
                ].astype(f32)
                bell = jnp.exp2(u * u * -LOG2_E)
                slope = 1.0 + (lax.erf(u) + (u * TWO_OVER_ROOT_PI) * bell)
                value = cot_refs[xl][0, 0, channel].astype(f32) * slope
                delta_ref[sub % 2, pair, g * Y : (g + 1) * Y, h * 128 : (h + 1) * 128] = value.astype(bf16)

    def lhs_of(slot):
        return lambda pair, groups: delta_ref[slot, pair, groups[0] * Y : (groups[-1] + 1) * Y, :]

    @pl.when(step == 0)
    def _():
        mixed_f32[...] = mixed_ref[...].astype(f32)
        for g in range(G):
            wave(0, 0, g)

    for sub in range(SUB):
        at = step * SUB + sub
        before = jnp.maximum(at - 1, 0)
        after = jnp.minimum(at + 1, XP - 1)
        slot = sub % 2
        lhs = lhs_of(1 - slot)
        spectral = [mm(wave_ref[slot], iz_ref[0])]
        totals = []
        for pair in range(4):
            if pair < 3:
                spectral.append(mm(wave_ref[slot], iz_ref[pair + 1]))
            delta(sub, pair, spectral[pair])
            if pair < 2:
                totals.append(z_transform(lhs, fz_ref, HALVES[pair]))
            else:
                for k, g in enumerate(HALVES[pair - 2]):
                    y_transform(totals[pair - 2][k * Y : (k + 1) * Y], fy_ref, modes_ref, g, before)
            for g in ((0, 1), (2,), (3,), (4,))[pair]:
                wave(after, 1 - slot, g)

    @pl.when(step == XP // SUB - 1)
    def _():
        lhs = lhs_of((SUB - 1) % 2)
        for groups in HALVES:
            analyse(lhs, fz_ref, fy_ref, modes_ref, XP - 1, groups)
        out_ref[...] = modes_ref[...].astype(bf16)


def slab_call(conv, cotangent, mixed, t):
    return pl.pallas_call(
        slab_kernel,
        out_shape=jax.ShapeDtypeStruct((2560, 128), bf16),
        grid=(XP // SUB,),
        in_specs=[
            *[pl.BlockSpec((1, C, Y, Z), lambda i: (i, 0, 0, 0))] * (2 * SUB),
            *x_streams(),
            full((2560, 128)),
            full((256, 128)),
            full((4, 256, 256)),
            full((4, 256, 256)),
            full((128, 256)),
        ],
        out_specs=pl.BlockSpec((2560, 128), lambda i: (0, 0)),
        scratch_shapes=[
            pltpu.VMEM((2560, 128), f32),
            pltpu.VMEM((2560, 128), f32),
            pltpu.VMEM((SUB, 640, 256), bf16),
            pltpu.VMEM((SUB, 4, 640, 256), bf16),
        ],
        compiler_params=pltpu.CompilerParams(
            dimension_semantics=("arbitrary",), vmem_limit_bytes=44 << 20
        ),
        name="slab",
    )(
        *map(in_hbm, [*conv, *[cotangent] * (2 * SUB)]), mixed, t["inverse_y"], t["inverse_z"],
        t["forward_z"], t["forward_y"],
    )


def small_call(kernel, name, out_shape, scratch, *args):
    return pl.pallas_call(
        kernel,
        out_shape=out_shape,
        scratch_shapes=scratch,
        compiler_params=pltpu.CompilerParams(vmem_limit_bytes=10 << 20),
        name=name,
    )(*args)


def lower_half():
    return lax.broadcasted_iota(jnp.int32, (64, 128), 1) < 64


def forward_x_kernel(in_ref, fx_ref, un_ref, out_ref, wide_ref):
    low = lower_half()
    for gk in range(GA):
        cols = []
        for b in range(2):
            row = (2 * gk + b) * 16
            cols.append(jnp.concatenate([in_ref[j * 320 + row : j * 320 + row + 16, :] for j in range(8)], axis=0))
        right = jnp.concatenate(cols, axis=1)
        out = mm(fx_ref[...], jnp.concatenate([right, right], axis=0))
        first = jnp.where(low, out[:64, :128], out[64:, 128:])
        second = jnp.where(low, out[:64, 128:], out[64:, :128])
        res = (first + pltpu.roll(second, 64, 1)) * un_ref[...]
        for r in range(4):
            wide_ref[pl.ds(r * GA + gk, 16, stride=40), :] = res[r * 16 : (r + 1) * 16]
    out_ref[...] = wide_ref[...].astype(bf16)


def inverse_x_kernel(in_ref, ix_ref, un_ref, out_ref, wide_ref):
    wide_ref[...] = in_ref[...].astype(f32)
    low = lax.broadcasted_iota(jnp.int32, (128, 128), 1) < 64
    for gk in range(GA):
        rows = [wide_ref[pl.ds(r * GA + gk, 16, stride=40), :] for r in range(4)]
        part = jnp.concatenate(rows, axis=0).astype(bf16)
        out = mm(ix_ref[...], jnp.concatenate([part, part], axis=0)) * un_ref[...]
        first = jnp.where(low, out[:128], pltpu.roll(out[128:], 64, 1)).astype(bf16)
        second = jnp.where(low, pltpu.roll(out[:128], 64, 1), out[128:]).astype(bf16)
        for b, value in enumerate((first, second)):
            row = (2 * gk + b) * 16
            for j in range(8):
                out_ref[j * 320 + row : j * 320 + row + 16, :] = value[j * 16 : (j + 1) * 16]


def weight_kernel(w_ref, place_ref, out_ref, wide_ref):
    wide_ref[...] = w_ref[...].astype(f32)
    cols = [wide_ref[pl.ds(o, 400, stride=4), :].astype(bf16) for o in range(4)]
    out = mm(jnp.concatenate(cols, axis=1), place_ref[...])
    out_ref[0] = out[:, :128]
    out_ref[1] = out[:, 128:]


def spread_channels(in_ref, spread_ref, wide_ref, rows_ref, chan_ref):
    wide_ref[...] = in_ref[...].astype(f32)
    for r in range(40):
        rows_ref[r * 16 : (r + 1) * 16, :] = wide_ref[pl.ds(r, 16, stride=40), :].astype(bf16)
    chan_ref[...] = mm(rows_ref[...], spread_ref[...])


def channel_parts(chan_ref, kxl, kya, c):
    row = (kxl * 20 + (c // 4) * 2 + kya) * 16
    lanes = (c % 4) * 128
    return (
        chan_ref[row : row + 16, lanes : lanes + 128],
        chan_ref[row + 160 : row + 176, lanes : lanes + 128],
    )


SPREAD_SCRATCH = (
    pltpu.VMEM((640, 128), f32), pltpu.VMEM((640, 128), bf16), pltpu.VMEM((640, 512), f32)
)


def mix_kernel(in_ref, spread_ref, w_ref, out_ref, wide_ref, rows_ref, chan_ref):
    spread_channels(in_ref, spread_ref, wide_ref, rows_ref, chan_ref)
    for kxl in range(2):
        for kya in range(2):
            real = [jnp.zeros((16, 128), f32) for _ in range(G)]
            imag = [jnp.zeros((16, 128), f32) for _ in range(G)]
            for c in range(C):
                s_re, s_im = channel_parts(chan_ref, kxl, kya, c)
                for go in range(G):
                    line = kxl * 200 + c * G + go
                    w_re = w_ref[kya, line : line + 1, :]
                    w_im = w_ref[kya, line + 100 : line + 101, :]
                    real[go] = real[go] + (s_re * w_re - s_im * w_im)
                    imag[go] = imag[go] + (s_re * w_im + s_im * w_re)
            for go in range(G):
                row = kxl * 20 + go * 2 + kya
                wide_ref[pl.ds(row, 16, stride=40), :] = real[go]
                wide_ref[pl.ds(row + 10, 16, stride=40), :] = imag[go]
    out_ref[...] = wide_ref[...].astype(bf16)


def grad_kernel(
    s_ref, b_ref, spread_ref, gather_ref, out_ref, wide_ref, rows_ref, chan_ref, line_ref, sum_ref
):
    spread_channels(s_ref, spread_ref, wide_ref, rows_ref, chan_ref)
    for r in range(40):
        for c4 in range(4):
            kxl, part, g, kya = r // 20, r // 10 % 2, r // 2 % 5, r % 2
            first = ((kxl * 2 + part) * 2 + kya) * 384 + 4 * g + c4
            line_ref[pl.ds(first, 16, stride=24), :] = chan_ref[
                r * 16 : (r + 1) * 16, c4 * 128 : (c4 + 1) * 128
            ]
    wide_ref[...] = b_ref[...].astype(f32)
    for kxl in range(2):
        for kya in range(2):
            base = (kxl * 4 + kya) * 384
            for go in range(G):
                real = jnp.zeros((24, 128), f32)
                imag = jnp.zeros((24, 128), f32)
                for s in range(DP):
                    row = s * 40 + kxl * 20 + go * 2 + kya
                    b_re = wide_ref[row : row + 1, :]
                    b_im = wide_ref[row + 10 : row + 11, :]
                    s_re = line_ref[base + s * 24 : base + s * 24 + 24, :]
                    s_im = line_ref[base + 768 + s * 24 : base + 768 + s * 24 + 24, :]
                    real = real + (s_re * b_re + s_im * b_im)
                    imag = imag + (s_re * b_im - s_im * b_re)
                first = kya * 400 + kxl * 100 + go
                sum_ref[pl.ds(first, C, stride=G), :] = real[:C]
                sum_ref[pl.ds(first + 200, C, stride=G), :] = imag[:C]
    sums = jnp.concatenate([sum_ref[:400, :], sum_ref[400:800, :]], axis=1)
    upper = sums.astype(bf16)
    lower = (sums - upper.astype(f32)).astype(bf16)
    placed = mm(jnp.concatenate([upper, lower], axis=1), gather_ref[...])
    for o in range(4):
        for part in range(2):
            line_ref[pl.ds(o * 2 + part, 200, stride=8), :] = placed[
                part * 200 : (part + 1) * 200, o * 128 : o * 128 + 128
            ]
    out_ref[...] = line_ref[:1600, :64]


def exchange(values, axis, count):
    blocks = values.reshape(count, -1, 128)
    return lax.all_to_all(blocks, axis, split_axis=0, concat_axis=0, tiled=True).reshape(-1, 128)


def shards(fields, cotangent, spectral_weight, conv_weight, conv_bias):
    t = {name: jnp.asarray(value) for name, value in tables().items()}
    def to_kx(moved, unscale):
        return small_call(
            forward_x_kernel, "forward_x", jax.ShapeDtypeStruct((640, 128), bf16),
            [pltpu.VMEM((640, 128), f32)], moved, t["forward_x"], unscale,
        )

    moved = exchange(analyse_call(fields, t), "mp", MP)
    moved, spectral_weight = lax.optimization_barrier((moved, spectral_weight))
    spectra = exchange(to_kx(moved, t["unscale"]), "dp", DP)
    weights = small_call(
        weight_kernel, "weights", jax.ShapeDtypeStruct((2, 400, 128), f32),
        [pltpu.VMEM((1600, 64), f32)], spectral_weight.reshape(1600, 64), t["place"],
    )
    mixed = small_call(
        mix_kernel, "mix", jax.ShapeDtypeStruct((640, 128), bf16), SPREAD_SCRATCH,
        spectra, t["spread"], weights,
    )
    slabs = small_call(
        inverse_x_kernel, "inverse_x", jax.ShapeDtypeStruct((2560, 128), bf16),
        [pltpu.VMEM((640, 128), f32)], exchange(mixed, "dp", DP), t["inverse_x"], t["unscale_inverse"],
    )
    slabs, conv_weight = lax.optimization_barrier((slabs, conv_weight))
    conv_term = conv_call(fields, conv_weight, conv_bias)
    back_modes = slab_call(conv_term, cotangent, exchange(slabs, "mp", MP), t)
    back = exchange(to_kx(exchange(back_modes, "mp", MP), t["unscale_back"]), "dp", DP)
    grad = small_call(
        grad_kernel, "grad", jax.ShapeDtypeStruct((1600, 64), f32),
        (*SPREAD_SCRATCH, pltpu.VMEM((3072, 128), f32), pltpu.VMEM((840, 128), f32)), spectra, back, t["spread"], t["gather"],
    )
    return jnp.transpose(grad.reshape(2, C, C, 2, 64), (0, 3, 1, 2, 4))


def solution(mesh):
    return jax.shard_map(
        shards,
        mesh=mesh,
        in_specs=(
            P("dp", "mp", None, None, None),
            P("dp", "mp", None, None, None),
            P("dp", None, None, None, "mp"),
            P(),
            P(),
        ),
        out_specs=P("dp", None, None, None, "mp"),
        check_vma=False,
    )
```

```python
import functools

import jax
import jax.numpy as jnp
import ml_dtypes
import numpy as np
from jax import lax
from jax.experimental import pallas as pl
from jax.experimental.pallas import tpu as pltpu
from jax.sharding import PartitionSpec as P

X = 128
Y = 128
Z = 128
C = 20
KX = 32
KY = 32
KZ = 16
DP = 16
MP = 8
XP = 8
G = 5
GK = 20
GA = 10
SUB = 2

bf16 = jnp.bfloat16
f32 = jnp.float32
np_bf16 = ml_dtypes.bfloat16

INV_ROOT_TWO = 0.7071067811865476
TWO_OVER_ROOT_PI = 1.1283791670955126
LOG2_E = 1.4426950408889634


def kept(count, length):
    return np.concatenate([np.arange(count // 2), np.arange(length - count // 2, length)])


def angles(modes, length):
    return 2.0 * np.pi / length * ((modes[:, None] * np.arange(length)[None, :]) % length)


def hi_lo(table):
    upper = table.astype(np_bf16)
    lower = (table - upper.astype(np.float64)).astype(np_bf16)
    return upper, lower


def z_scales():
    candidates = 1.0 + np.arange(512) / 512
    scales = []
    for row in angles(np.arange(KZ), Z):
        values = np.concatenate([np.cos(row), np.sin(row)])[None, :] * candidates[:, None]
        off = ((values.astype(np_bf16).astype(np.float64) - values) ** 2).sum(1) / (values**2).sum(1)
        scales.append(candidates[int(np.argmin(off))])
    return np.array(scales)


@functools.cache
def tables():
    scale = z_scales()
    weight = np.where(np.arange(KZ) == 0, 1.0, 2.0) / (X * Y * Z)
    phase_z = angles(np.arange(KZ), Z)
    cos_z, sin_z = np.cos(phase_z), np.sin(phase_z)
    forward_z = np.zeros((8, Z, 2, 8, KZ))
    inverse_z = np.zeros((4, 2, 8, KZ, 2, Z))
    for q in range(8):
        forward_z[q, :, 0, q, :] = (cos_z * scale[:, None]).T
        forward_z[q, :, 1, q, :] = (sin_z * scale[:, None]).T
        inverse_z[q // 2, 0, q, :, q % 2, :] = cos_z * scale[:, None]
        inverse_z[q // 2, 1, q, :, q % 2, :] = -sin_z * scale[:, None]
    unscale = np.tile(1.0 / scale, 8)[None, :]
    unscale_back = np.tile(0.5 * weight / scale, 8)[None, :]
    unscale_inverse = np.tile(INV_ROOT_TWO * weight / scale, 8)[None, :]
    phase_y = angles(kept(KY, Y), Y)
    cos_y, sin_y = np.cos(phase_y), np.sin(phase_y)
    forward_y = np.zeros((KY, 2, 2, Y))
    forward_y[:, 0, 0], forward_y[:, 0, 1] = cos_y, -sin_y
    forward_y[:, 1, 0], forward_y[:, 1, 1] = -sin_y, -cos_y
    forward_y = np.concatenate(hi_lo(forward_y.reshape(64, 256)), axis=0)
    inverse_y = np.zeros((2, Y, KY, 2))
    inverse_y[0, :, :, 0], inverse_y[0, :, :, 1] = cos_y.T, -sin_y.T
    inverse_y[1, :, :, 0], inverse_y[1, :, :, 1] = sin_y.T, cos_y.T
    inverse_y = np.concatenate(hi_lo(inverse_y.reshape(256, 64)), axis=1)
    phase_x = angles(kept(KX, X), X).reshape(16, 2, 8, 8, 2)
    cos_x, sin_x = np.cos(phase_x), np.sin(phase_x)
    forward_x = np.zeros((2, 2, 2, 16, 8, 2, 8))
    inverse_x = np.zeros((2, 8, 2, 8, 2, 2, 16))
    cos_f = np.transpose(cos_x, (4, 1, 0, 2, 3))
    sin_f = np.transpose(sin_x, (4, 1, 0, 2, 3))
    forward_x[:, :, 0, :, :, 0, :] = cos_f
    forward_x[:, :, 0, :, :, 1, :] = sin_f
    forward_x[:, :, 1, :, :, 0, :] = -sin_f
    forward_x[:, :, 1, :, :, 1, :] = cos_f
    cos_i = np.transpose(cos_x, (4, 2, 3, 1, 0))
    sin_i = np.transpose(sin_x, (4, 2, 3, 1, 0))
    inverse_x[:, :, 0, :, :, 0, :] = cos_i
    inverse_x[:, :, 0, :, :, 1, :] = -sin_i
    inverse_x[:, :, 1, :, :, 0, :] = sin_i
    inverse_x[:, :, 1, :, :, 1, :] = cos_i
    forward_x = np.concatenate(hi_lo(forward_x.reshape(128, 128)), axis=1)
    inverse_x = np.concatenate(hi_lo(inverse_x.reshape(256, 64)), axis=1)
    spread = np.zeros((2, 4, KZ, 4, 2, 4, KZ))
    for channel in range(4):
        for place in range(4):
            for b in range(2):
                spread[b, channel, np.arange(KZ), channel, b, place, np.arange(KZ)] = 1.0
    spread = spread.reshape(128, 512)
    place = np.zeros((4, 4, KZ, 2, 2, 4, KZ))
    for o in range(4):
        for kyl in range(4):
            place[o, kyl, np.arange(KZ), kyl // 2, kyl % 2, o, np.arange(KZ)] = 1.0
    gather = np.zeros((2, 2, 4, KZ, 4, 2, 2, 2, KZ))
    for o in range(4):
        for a in range(2):
            for b in range(2):
                gather[a, b, o, np.arange(KZ), o, 0, a, b, np.arange(KZ)] = 1.0
    gather = gather.reshape(256, 512)
    return dict(
        gather=np.concatenate([gather, gather], axis=0).astype(np_bf16),
        forward_z=forward_z.reshape(4, 256, 256).astype(np_bf16),
        inverse_z=inverse_z.reshape(4, 256, 256).astype(np_bf16),
        unscale=unscale.astype(np.float32),
        unscale_back=unscale_back.astype(np.float32),
        unscale_inverse=unscale_inverse.astype(np.float32),
        forward_y=forward_y,
        inverse_y=inverse_y,
        forward_x=forward_x,
        inverse_x=inverse_x,
        spread=spread.astype(np_bf16),
        place=place.reshape(256, 256).astype(np_bf16),
    )


def mm(a, b):
    return jnp.dot(a, b, preferred_element_type=f32)


def z_transform(lhs_of, fz_ref, groups):
    total = mm(lhs_of(0, groups), fz_ref[0])
    for pair in range(1, 4):
        total = total + mm(lhs_of(pair, groups), fz_ref[pair])
    return total


def y_transform(part, fy_ref, modes_ref, g, at):
    both = jnp.concatenate([part[:, :128], part[:, 128:]], axis=0)
    upper = both.astype(bf16)
    lower = (both - upper.astype(f32)).astype(bf16)
    out = mm(fy_ref[...], jnp.concatenate([upper, lower], axis=1))
    modes = out[:64, :128] + out[64:, :128] + out[:64, 128:]
    for j in range(MP):
        modes_ref[pl.ds(j * 320 + g * 64 + at, 8, stride=8), :] = modes[j * 8 : (j + 1) * 8]


def analyse(lhs_of, fz_ref, fy_ref, modes_ref, at, groups):
    total = z_transform(lhs_of, fz_ref, groups)
    for k, g in enumerate(groups):
        y_transform(total[k * Y : (k + 1) * Y], fy_ref, modes_ref, g, at)


HALVES = ((0, 1, 2), (3, 4))


def analyse_kernel(*refs):
    field_refs, (fz_ref, fy_ref, out_ref, modes_ref) = refs[: 2 * SUB], refs[2 * SUB :]
    step = pl.program_id(0)

    def lhs_of(sub):
        def lhs(pair, groups):
            xl, c4 = 2 * sub + pair // 2, 2 * (pair % 2)
            rows = [
                jnp.concatenate(
                    [field_refs[xl][0, 0, 4 * g + c4], field_refs[xl][0, 0, 4 * g + c4 + 1]], axis=1
                )
                for g in groups
            ]
            return jnp.concatenate(rows, axis=0)

        return lhs

    totals = [z_transform(lhs_of(sub), fz_ref, range(G)) for sub in range(SUB)]
    for g in range(G):
        for sub in range(SUB):
            y_transform(totals[sub][g * Y : (g + 1) * Y], fy_ref, modes_ref, g, step * SUB + sub)

    @pl.when(step == XP // SUB - 1)
    def _():
        out_ref[...] = modes_ref[...].astype(bf16)


def x_streams():
    return [
        pl.BlockSpec((1, 1, C, Y, Z), lambda i, k=k: (0, 2 * SUB * i + k, 0, 0, 0))
        for k in range(2 * SUB)
    ]


def in_hbm(array):
    return pltpu.with_memory_space_constraint(array, pltpu.HBM)


def full(shape):
    zeros = (0,) * len(shape)
    return pl.BlockSpec(shape, lambda *_: zeros, pipeline_mode=pl.Buffered(1))


def analyse_call(fields, t):
    return pl.pallas_call(
        analyse_kernel,
        out_shape=jax.ShapeDtypeStruct((2560, 128), bf16),
        grid=(XP // SUB,),
        in_specs=[
            *x_streams(),
            full((4, 256, 256)),
            full((128, 256)),
        ],
        out_specs=pl.BlockSpec((2560, 128), lambda i: (0, 0)),
        scratch_shapes=[pltpu.VMEM((2560, 128), f32)],
        compiler_params=pltpu.CompilerParams(
            dimension_semantics=("arbitrary",), vmem_limit_bytes=44 << 20
        ),
        name="analyse",
    )(*map(in_hbm, [*[fields] * (2 * SUB), t["forward_z"], t["forward_y"]]))


def conv_kernel(*refs):
    field_refs, (w_ref, bias_ref) = refs[: 2 * SUB], refs[2 * SUB : 2 * SUB + 2]
    out_refs, (conv_ref, lines_ref) = refs[2 * SUB + 2 : 4 * SUB + 2], refs[4 * SUB + 2 :]

    @pl.when(pl.program_id(0) == 0)
    def _():
        def picks(shape, along):
            long = lax.broadcasted_iota(jnp.int32, shape, along) >> 4
            return jnp.where(long == lax.broadcasted_iota(jnp.int32, shape, 1 - along), 1.0, 0.0).astype(bf16)

        by_row = lax.dot_general(
            picks((320, C), 0), w_ref[...], (((1,), (1,)), ((), ())), preferred_element_type=f32
        ).astype(bf16)
        spread = mm(by_row, picks((C, 320), 1))
        row = lax.broadcasted_iota(jnp.int32, (320, 320), 0) & 15
        column = lax.broadcasted_iota(jnp.int32, (320, 320), 1) & 15
        conv_ref[...] = jnp.where(row == column, spread, 0.0).astype(bf16)
        for o in range(C):
            lines_ref[o * 16 : (o + 1) * 16, :] = jnp.full((16, 256), bias_ref[o], f32)

    bias = lines_ref[...]
    for xl in range(2 * SUB):
        for yp in range(4):
            right = jnp.concatenate(
                [
                    field_refs[xl][0, 0, :, yp * 32 + h * 16 : yp * 32 + (h + 1) * 16, :].reshape(320, Z)
                    for h in range(2)
                ],
                axis=1,
            )
            out = ((mm(conv_ref[...], right) + bias) * INV_ROOT_TWO).astype(bf16)
            for h in range(2):
                out_refs[xl][0, :, yp * 32 + h * 16 : yp * 32 + (h + 1) * 16, :] = out[
                    :, h * 128 : (h + 1) * 128
                ].reshape(C, 16, Z)


def conv_call(fields, conv, bias):
    return pl.pallas_call(
        conv_kernel,
        out_shape=[pltpu.HBM((XP // SUB, C, Y, Z), bf16)] * (2 * SUB),
        grid=(XP // SUB,),
        in_specs=[
            *x_streams(),
            full((C, C)),
            pl.BlockSpec(memory_space=pltpu.SMEM),
        ],
        out_specs=[pl.BlockSpec((1, C, Y, Z), lambda i: (i, 0, 0, 0))] * (2 * SUB),
        scratch_shapes=[pltpu.VMEM((320, 320), bf16), pltpu.VMEM((320, 256), f32)],
        compiler_params=pltpu.CompilerParams(
            dimension_semantics=("arbitrary",), vmem_limit_bytes=44 << 20
        ),
        cost_estimate=pl.CostEstimate(
            flops=2 * 16 * Y * Z * 320 * C, bytes_accessed=4 * 16 * C * Y * Z, transcendentals=0
        ),
        name="conv",
    )(*map(in_hbm, [fields] * (2 * SUB)), conv, bias)


def slab_kernel(*refs):
    conv_refs, cot_refs = refs[: 2 * SUB], refs[2 * SUB : 4 * SUB]
    mixed_ref, iy_ref, iz_ref, fz_ref, fy_ref, out_ref = refs[4 * SUB : 4 * SUB + 6]
    modes_ref, mixed_f32, wave_ref, delta_ref = refs[4 * SUB + 6 :]
    step = pl.program_id(0)

    def wave(at, slot, g):
        rows = [mixed_f32[pl.ds(j * 320 + g * 64 + at, 8, stride=8), :] for j in range(MP)]
        part = jnp.concatenate(rows, axis=0).astype(bf16)
        out = mm(iy_ref[...], jnp.concatenate([part, part], axis=0))
        out = out.astype(bf16)
        wave_ref[slot, g * Y : (g + 1) * Y, :128] = out[:Y]
        wave_ref[slot, g * Y : (g + 1) * Y, 128:] = out[Y:]

    def delta(sub, pair, spectral):
        xl = 2 * sub + pair // 2
        for g in range(G):
            for h in range(2):
                channel = 4 * g + 2 * (pair % 2) + h
                u = spectral[g * Y : (g + 1) * Y, h * 128 : (h + 1) * 128] + conv_refs[xl][
                    0, channel
                ].astype(f32)
                bell = jnp.exp2(u * u * -LOG2_E)
                slope = 1.0 + (lax.erf(u) + (u * TWO_OVER_ROOT_PI) * bell)
                value = cot_refs[xl][0, 0, channel].astype(f32) * slope
                delta_ref[sub % 2, pair, g * Y : (g + 1) * Y, h * 128 : (h + 1) * 128] = value.astype(bf16)

    def lhs_of(slot):
        return lambda pair, groups: delta_ref[slot, pair, groups[0] * Y : (groups[-1] + 1) * Y, :]

    @pl.when(step == 0)
    def _():
        mixed_f32[...] = mixed_ref[...].astype(f32)
        for g in range(G):
            wave(0, 0, g)

    for sub in range(SUB):
        at = step * SUB + sub
        before = jnp.maximum(at - 1, 0)
        after = jnp.minimum(at + 1, XP - 1)
        slot = sub % 2
        lhs = lhs_of(1 - slot)
        spectral = [mm(wave_ref[slot], iz_ref[0])]
        totals = []
        for pair in range(4):
            if pair < 3:
                spectral.append(mm(wave_ref[slot], iz_ref[pair + 1]))
            delta(sub, pair, spectral[pair])
            if pair < 2:
                totals.append(z_transform(lhs, fz_ref, HALVES[pair]))
            else:
                for k, g in enumerate(HALVES[pair - 2]):
                    y_transform(totals[pair - 2][k * Y : (k + 1) * Y], fy_ref, modes_ref, g, before)
            for g in ((0, 1), (2,), (3,), (4,))[pair]:
                wave(after, 1 - slot, g)

    @pl.when(step == XP // SUB - 1)
    def _():
        lhs = lhs_of((SUB - 1) % 2)
        for groups in HALVES:
            analyse(lhs, fz_ref, fy_ref, modes_ref, XP - 1, groups)
        out_ref[...] = modes_ref[...].astype(bf16)


def slab_call(conv, cotangent, mixed, t):
    return pl.pallas_call(
        slab_kernel,
        out_shape=jax.ShapeDtypeStruct((2560, 128), bf16),
        grid=(XP // SUB,),
        in_specs=[
            *[pl.BlockSpec((1, C, Y, Z), lambda i: (i, 0, 0, 0))] * (2 * SUB),
            *x_streams(),
            full((2560, 128)),
            full((256, 128)),
            full((4, 256, 256)),
            full((4, 256, 256)),
            full((128, 256)),
        ],
        out_specs=pl.BlockSpec((2560, 128), lambda i: (0, 0)),
        scratch_shapes=[
            pltpu.VMEM((2560, 128), f32),
            pltpu.VMEM((2560, 128), f32),
            pltpu.VMEM((SUB, 640, 256), bf16),
            pltpu.VMEM((SUB, 4, 640, 256), bf16),
        ],
        compiler_params=pltpu.CompilerParams(
            dimension_semantics=("arbitrary",), vmem_limit_bytes=44 << 20
        ),
        name="slab",
    )(
        *map(in_hbm, [*conv, *[cotangent] * (2 * SUB)]), mixed, t["inverse_y"], t["inverse_z"],
        t["forward_z"], t["forward_y"],
    )


def small_call(kernel, name, out_shape, scratch, *args):
    return pl.pallas_call(
        kernel,
        out_shape=out_shape,
        scratch_shapes=scratch,
        compiler_params=pltpu.CompilerParams(vmem_limit_bytes=10 << 20),
        name=name,
    )(*args)


def lower_half():
    return lax.broadcasted_iota(jnp.int32, (64, 128), 1) < 64


def forward_x_kernel(in_ref, fx_ref, un_ref, out_ref, wide_ref):
    low = lower_half()
    for gk in range(GA):
        cols = []
        for b in range(2):
            row = (2 * gk + b) * 16
            cols.append(jnp.concatenate([in_ref[j * 320 + row : j * 320 + row + 16, :] for j in range(8)], axis=0))
        right = jnp.concatenate(cols, axis=1)
        out = mm(fx_ref[...], jnp.concatenate([right, right], axis=0))
        first = jnp.where(low, out[:64, :128], out[64:, 128:])
        second = jnp.where(low, out[:64, 128:], out[64:, :128])
        res = (first + pltpu.roll(second, 64, 1)) * un_ref[...]
        for r in range(4):
            wide_ref[pl.ds(r * GA + gk, 16, stride=40), :] = res[r * 16 : (r + 1) * 16]
    out_ref[...] = wide_ref[...].astype(bf16)


def inverse_x_kernel(in_ref, ix_ref, un_ref, out_ref, wide_ref):
    wide_ref[...] = in_ref[...].astype(f32)
    low = lax.broadcasted_iota(jnp.int32, (128, 128), 1) < 64
    for gk in range(GA):
        rows = [wide_ref[pl.ds(r * GA + gk, 16, stride=40), :] for r in range(4)]
        part = jnp.concatenate(rows, axis=0).astype(bf16)
        out = mm(ix_ref[...], jnp.concatenate([part, part], axis=0)) * un_ref[...]
        first = jnp.where(low, out[:128], pltpu.roll(out[128:], 64, 1)).astype(bf16)
        second = jnp.where(low, pltpu.roll(out[:128], 64, 1), out[128:]).astype(bf16)
        for b, value in enumerate((first, second)):
            row = (2 * gk + b) * 16
            for j in range(8):
                out_ref[j * 320 + row : j * 320 + row + 16, :] = value[j * 16 : (j + 1) * 16]


def weight_kernel(w_ref, place_ref, out_ref, wide_ref):
    wide_ref[...] = w_ref[...].astype(f32)
    cols = [wide_ref[pl.ds(o, 400, stride=4), :].astype(bf16) for o in range(4)]
    out = mm(jnp.concatenate(cols, axis=1), place_ref[...])
    out_ref[0] = out[:, :128]
    out_ref[1] = out[:, 128:]


def spread_channels(in_ref, spread_ref, wide_ref, rows_ref, chan_ref):
    wide_ref[...] = in_ref[...].astype(f32)
    for r in range(40):
        rows_ref[r * 16 : (r + 1) * 16, :] = wide_ref[pl.ds(r, 16, stride=40), :].astype(bf16)
    chan_ref[...] = mm(rows_ref[...], spread_ref[...])


def channel_parts(chan_ref, kxl, kya, c):
    row = (kxl * 20 + (c // 4) * 2 + kya) * 16
    lanes = (c % 4) * 128
    return (
        chan_ref[row : row + 16, lanes : lanes + 128],
        chan_ref[row + 160 : row + 176, lanes : lanes + 128],
    )


SPREAD_SCRATCH = (
    pltpu.VMEM((640, 128), f32), pltpu.VMEM((640, 128), bf16), pltpu.VMEM((640, 512), f32)
)


def mix_kernel(in_ref, spread_ref, w_ref, out_ref, wide_ref, rows_ref, chan_ref):
    spread_channels(in_ref, spread_ref, wide_ref, rows_ref, chan_ref)
    for kxl in range(2):
        for kya in range(2):
            real = [jnp.zeros((16, 128), f32) for _ in range(G)]
            imag = [jnp.zeros((16, 128), f32) for _ in range(G)]
            for c in range(C):
                s_re, s_im = channel_parts(chan_ref, kxl, kya, c)
                for go in range(G):
                    line = kxl * 200 + c * G + go
                    w_re = w_ref[kya, line : line + 1, :]
                    w_im = w_ref[kya, line + 100 : line + 101, :]
                    real[go] = real[go] + (s_re * w_re - s_im * w_im)
                    imag[go] = imag[go] + (s_re * w_im + s_im * w_re)
            for go in range(G):
                row = kxl * 20 + go * 2 + kya
                wide_ref[pl.ds(row, 16, stride=40), :] = real[go]
                wide_ref[pl.ds(row + 10, 16, stride=40), :] = imag[go]
    out_ref[...] = wide_ref[...].astype(bf16)


def grad_kernel(
    s_ref, b_ref, spread_ref, gather_ref, out_ref, wide_ref, rows_ref, chan_ref, line_ref, sum_ref
):
    spread_channels(s_ref, spread_ref, wide_ref, rows_ref, chan_ref)
    for r in range(40):
        for c4 in range(4):
            kxl, part, g, kya = r // 20, r // 10 % 2, r // 2 % 5, r % 2
            first = ((kxl * 2 + part) * 2 + kya) * 384 + 4 * g + c4
            line_ref[pl.ds(first, 16, stride=24), :] = chan_ref[
                r * 16 : (r + 1) * 16, c4 * 128 : (c4 + 1) * 128
            ]
    wide_ref[...] = b_ref[...].astype(f32)
    for kxl in range(2):
        for kya in range(2):
            base = (kxl * 4 + kya) * 384
            real = [jnp.zeros((24, 128), f32) for _ in range(G)]
            imag = [jnp.zeros((24, 128), f32) for _ in range(G)]
            for s in range(DP):
                s_re = line_ref[base + s * 24 : base + s * 24 + 24, :]
                s_im = line_ref[base + 768 + s * 24 : base + 768 + s * 24 + 24, :]
                for go in range(G):
                    row = s * 40 + kxl * 20 + go * 2 + kya
                    b_re = wide_ref[row : row + 1, :]
                    b_im = wide_ref[row + 10 : row + 11, :]
                    real[go] = real[go] + (s_re * b_re + s_im * b_im)
                    imag[go] = imag[go] + (s_re * b_im - s_im * b_re)
            for go in range(G):
                first = kya * 400 + kxl * 100 + go
                sum_ref[pl.ds(first, C, stride=G), :] = real[go][:C]
                sum_ref[pl.ds(first + 200, C, stride=G), :] = imag[go][:C]
    sums = jnp.concatenate([sum_ref[:400, :], sum_ref[400:800, :]], axis=1)
    upper = sums.astype(bf16)
    lower = (sums - upper.astype(f32)).astype(bf16)
    placed = mm(jnp.concatenate([upper, lower], axis=1), gather_ref[...])
    for o in range(4):
        for part in range(2):
            line_ref[pl.ds(o * 2 + part, 200, stride=8), :] = placed[
                part * 200 : (part + 1) * 200, o * 128 : o * 128 + 128
            ]
    out_ref[...] = line_ref[:1600, :64]


def exchange(values, axis, count):
    blocks = values.reshape(count, -1, 128)
    return lax.all_to_all(blocks, axis, split_axis=0, concat_axis=0, tiled=True).reshape(-1, 128)


def shards(fields, cotangent, spectral_weight, conv_weight, conv_bias):
    t = {name: jnp.asarray(value) for name, value in tables().items()}
    def to_kx(moved, unscale):
        return small_call(
            forward_x_kernel, "forward_x", jax.ShapeDtypeStruct((640, 128), bf16),
            [pltpu.VMEM((640, 128), f32)], moved, t["forward_x"], unscale,
        )

    moved = exchange(analyse_call(fields, t), "mp", MP)
    weights = small_call(
        weight_kernel, "weights", jax.ShapeDtypeStruct((2, 400, 128), f32),
        [pltpu.VMEM((1600, 64), f32)], spectral_weight.reshape(1600, 64), t["place"],
    )
    moved, weights = lax.optimization_barrier((moved, weights))
    spectra = exchange(to_kx(moved, t["unscale"]), "dp", DP)
    mixed = small_call(
        mix_kernel, "mix", jax.ShapeDtypeStruct((640, 128), bf16), SPREAD_SCRATCH,
        spectra, t["spread"], weights,
    )
    slabs = small_call(
        inverse_x_kernel, "inverse_x", jax.ShapeDtypeStruct((2560, 128), bf16),
        [pltpu.VMEM((640, 128), f32)], exchange(mixed, "dp", DP), t["inverse_x"], t["unscale_inverse"],
    )
    slabs, conv_weight = lax.optimization_barrier((slabs, conv_weight))
    conv_term = conv_call(fields, conv_weight, conv_bias)
    back_modes = slab_call(conv_term, cotangent, exchange(slabs, "mp", MP), t)
    back = exchange(to_kx(exchange(back_modes, "mp", MP), t["unscale_back"]), "dp", DP)
    grad = small_call(
        grad_kernel, "grad", jax.ShapeDtypeStruct((1600, 64), f32),
        (*SPREAD_SCRATCH, pltpu.VMEM((3072, 128), f32), pltpu.VMEM((840, 128), f32)), spectra, back, t["spread"], t["gather"],
    )
    return jnp.transpose(grad.reshape(2, C, C, 2, 64), (0, 3, 1, 2, 4))


def solution(mesh):
    return jax.shard_map(
        shards,
        mesh=mesh,
        in_specs=(
            P("dp", "mp", None, None, None),
            P("dp", "mp", None, None, None),
            P("dp", None, None, None, "mp"),
            P(),
            P(),
        ),
        out_specs=P("dp", None, None, None, "mp"),
        check_vma=False,
    )
```
